128 devices in a mesh: group: 8 (over z, x_lo), tensor: 16 (over y, x_hi, core).
Axes of the slice: x: 4 (x_hi: 2, x_lo: 2; x = x_hi * 2 + x_lo), y: 4, z: 4, core: 2. Of those that a mesh axis runs over, the one named last changes fastest.
Arguments:
- low_state: bfloat16 [4096, 8192], P('group', 'tensor'), may hold values from -6 to 6
- mid_state: bfloat16 [4096, 8192], P('group', 'tensor'), may hold values from -6 to 6
- residual: bfloat16 [4096, 8192], P('group', 'tensor'), may hold values from -6 to 6
- attention: bfloat16 [4096, 8192], P('group', 'tensor'), may hold values from -6 to 6
- o_weight: bfloat16 [8192, 8192], P('tensor'), may hold values from -0.0625 to 0.0625
- fc_weight: bfloat16 [3, 8192, 8192], P(None, 'tensor', 'group'), may hold values from -0.0390625 to 0.0390625
- norm_gain: float32 [8192], P('group'), may hold values from 0.1 to 1.9
- target: bfloat16 [2048, 8192], P('tensor', 'group'), may hold values from -6 to 6
- counts: int32 [8], replicated, may hold values from 32 to 256, as said below
- accept_rows: int32 [8, 512], replicated, may hold values from 0 to 511, each once within a row
- owners: int32 [8, 512], replicated, may hold values from 0 to 7, as said below
Outputs:
- top_state: bfloat16 [4096, 8192], P('group', 'tensor')
- fc_grad: float32 [3, 8192, 8192], P(None, 'tensor', 'group')
The draws below stay inside these ranges and needn't reach their ends.
Inputs may be any that keep to these rules, and one draw needn't show every extreme that they name: The counts sum to exactly 1024. Every replica accepts at least 32 rows, and in every draw one replica accepts 8 * 32. `accept_rows`: only the first counts[g] entries of row g are accepted rows. `owners`: among the first counts[g] entries of row g no shard appears more than 32 times; in every draw one shard receives exactly 32 rows from every replica, and the replica with the most accepted rows sends 32 to every shard. Later entries are unused.
All inputs are finite; a program needn't handle non-finite values.
Results may differ from the reference program's by a relative error of at most 0.012.
Values may be sent and summed in bfloat16 or wider, within the bound.
A program may use at most 128 MiB of HBM per device.

```python
import jax
import jax.numpy as jnp
from jax import lax

D = 8192
ROWS = 512
SLOTS = 32
ALL_ROWS = 4096
TRAIN_ROWS = 2048
ACCEPTED = 1024
N_GROUP = 8
N_TENSOR = 16


def routing_draw(key):
    base = jax.random.fold_in(key, 4711)
    keys = jax.random.split(base, 4)
    length = N_GROUP * SLOTS
    busiest = jax.random.randint(keys[1], (), 0, N_GROUP)
    is_busiest = jnp.arange(N_GROUP) == busiest
    weights = jnp.where(is_busiest, 0, jax.random.randint(keys[0], (N_GROUP,), 1, 3)).astype(jnp.int32)
    spare = ACCEPTED - length - (N_GROUP - 1) * SLOTS
    running = jnp.cumsum(weights).astype(jnp.int32)
    bounds = spare * running // running[-1]
    extras = bounds - jnp.concatenate([jnp.zeros((1,), jnp.int32), bounds[:-1]])
    counts = jnp.where(is_busiest, length, SLOTS + extras).astype(jnp.int32)
    full_owner = jax.random.randint(keys[2], (), 0, N_GROUP)
    labels = jnp.repeat(jnp.arange(N_GROUP, dtype=jnp.int32), SLOTS)
    position = jnp.arange(length, dtype=jnp.int32)

    def one_replica(replica_key, accepted):
        first_key, second_key, third_key = jax.random.split(replica_key, 3)
        noise = jax.random.randint(first_key, (length,), 1, 4096)
        score = jnp.where(labels == full_owner, 0, noise) * length + position
        ordered = labels[jnp.argsort(score)]
        mixing = jax.random.randint(second_key, (length,), 0, 4096)
        order_key = jnp.where(position < accepted, mixing, 4096) * length + position
        shuffled = ordered[jnp.argsort(order_key)]
        remainder = jax.random.randint(third_key, (ROWS - length,), 0, N_GROUP)
        return jnp.concatenate([shuffled, remainder.astype(jnp.int32)]).astype(jnp.int32)
    owners = jax.vmap(one_replica)(jax.random.split(keys[3], N_GROUP), counts)
    return (counts, owners)


def draw_counts(key, part):
    return routing_draw(key)[0]


def draw_owners(key, part):
    return routing_draw(key)[1]


def block_scale(stream_key, extent, pieces, low, top_value):
    loudness = 1.0
    for dim, blocks in pieces:
        heights = jax.random.uniform(jax.random.fold_in(jax.random.fold_in(stream_key, 6), dim), (blocks,), jnp.float32, low / len(pieces), top_value / len(pieces))
        loudness = loudness * jnp.repeat(jnp.exp(heights), extent[dim] // blocks).reshape((-1,) + (1,) * (len(extent) - 1 - dim))
    return loudness


def bell_draw(rng, shape, spread, limit, cuts=(), held_as=jnp.bfloat16):
    array = spread * jax.random.normal(rng, shape, jnp.float32)
    if cuts:
        array = array * block_scale(rng, shape, cuts, -0.22, 0.18)
    return jnp.clip(array, -limit, limit).astype(held_as)


def setup_inputs(seed: int = 0) -> dict:
    seeds = jax.random.split(jax.random.key(seed), 12)
    return {
        "low_state": bell_draw(seeds[0], (ALL_ROWS, D), 1.0, 6.0, ((0, 8), (1, 16))),
        "mid_state": bell_draw(seeds[1], (ALL_ROWS, D), 1.0, 6.0, ((0, 8), (1, 16))),
        "residual": bell_draw(seeds[2], (ALL_ROWS, D), 1.0, 6.0, ((0, 8), (1, 16))),
        "attention": bell_draw(seeds[3], (ALL_ROWS, D), 1.0, 6.0, ((0, 8), (1, 16))),
        "o_weight": bell_draw(seeds[4], (D, D), D ** -0.5, 0.0625, ((0, 16),)),
        "fc_weight": bell_draw(seeds[5], (3, D, D), (3 * D) ** -0.5, 0.0390625, ((1, 16), (2, 8))),
        "norm_gain": jnp.clip(1.0 + 0.18 * jax.random.normal(seeds[6], (D,), jnp.float32), 0.1, 1.9),
        "target": bell_draw(seeds[7], (TRAIN_ROWS, D), 1.0, 6.0, ((0, 16), (1, 8))),
        "counts": draw_counts(jax.random.fold_in(seeds[11], 71), 0),
        "accept_rows": jax.vmap(lambda own: jax.random.permutation(own, ROWS))(jax.random.split(seeds[9], N_GROUP)).reshape((N_GROUP, ROWS)).astype(jnp.int32),
        "owners": draw_owners(jax.random.fold_in(seeds[11], 71), 0),
    }


epsilon = 1e-05

def reference(low_state, mid_state, residual, attention, o_weight, fc_weight, norm_gain, target, counts, accept_rows, owners):
    width = D // N_TENSOR
    partial_total = jnp.zeros((N_GROUP * ROWS, D), jnp.float32)
    for block in range(N_TENSOR):
        term = jnp.dot(attention[:, block * width:(block + 1) * width], o_weight[block * width:(block + 1) * width], preferred_element_type=jnp.float32)
        rounded = lax.optimization_barrier(term.astype(jnp.bfloat16))
        partial_total = partial_total + rounded.astype(jnp.float32)
    top_state = (residual.astype(jnp.float32) + partial_total).astype(jnp.bfloat16)
    capacity = N_GROUP * SLOTS
    train_rows = N_GROUP * capacity
    live = jnp.arange(ROWS, dtype=jnp.int32)[None, :] < counts[:, None]
    onehot = ((owners[:, :, None] == jnp.arange(N_GROUP, dtype=jnp.int32)[None, None, :]) & live[:, :, None]).astype(jnp.int32)
    ranks = lax.optimization_barrier(jnp.sum((jnp.cumsum(onehot, axis=1) - onehot) * onehot, axis=2))
    replica = jnp.arange(N_GROUP, dtype=jnp.int32)[:, None]
    slot = jnp.where(live, owners * capacity + replica * SLOTS + ranks, train_rows).astype(jnp.int32)
    whole_row = (replica * ROWS + accept_rows).astype(jnp.int32)
    source = jnp.zeros((train_rows + 1,), jnp.int32).at[slot.reshape(-1)].set(whole_row.reshape(-1))[:train_rows]
    valid = jnp.zeros((train_rows + 1,), jnp.float32).at[slot.reshape(-1)].set(1.0)[:train_rows]
    states = jnp.concatenate([low_state, mid_state, top_state], axis=1)
    inputs = jnp.take(states, source, axis=0) * valid[:, None].astype(jnp.bfloat16)
    combined = jnp.dot(inputs, fc_weight.reshape(3 * D, D), preferred_element_type=jnp.float32)
    squares = lax.optimization_barrier(jnp.sum(combined * combined, axis=1))
    scale = lax.rsqrt(squares / D + epsilon)
    gain = norm_gain.astype(jnp.float32)
    normed = combined * scale[:, None] * gain[None, :]
    total = jnp.sum(counts).astype(jnp.float32)
    slope = valid[:, None] * (normed - target.astype(jnp.float32)) / total
    inner = lax.optimization_barrier(jnp.sum(gain[None, :] * slope * combined, axis=1))
    back = scale[:, None] * gain[None, :] * slope - combined * (scale ** 3 * inner / D)[:, None]
    back = back.astype(jnp.bfloat16)
    grad = jnp.dot(inputs.T, back, preferred_element_type=jnp.float32)
    return (top_state, grad.reshape(3, D, D))
```

```python
import functools

import jax
import jax.numpy as jnp
from jax import lax
from jax.experimental import pallas as pl
from jax.experimental.pallas import tpu as pltpu
from jax.sharding import PartitionSpec as P

D = 8192
SLOTS = 32
MESH = pl.DeviceIdType.MESH

epsilon = 1e-05


def row_plan(counts, accept_rows, owners, group_count, group_index, slots):
    rows = owners.shape[1]
    count = lax.dynamic_index_in_dim(counts, group_index, 0, keepdims=False)
    owner = lax.dynamic_index_in_dim(owners, group_index, 0, keepdims=False)
    accept = lax.dynamic_index_in_dim(accept_rows, group_index, 0, keepdims=False)
    index = jnp.arange(rows, dtype=jnp.int32)
    live = index < count
    earlier = (owner[None, :] == owner[:, None]) & (index[None, :] < index[:, None]) & live[None, :]
    ranks = jnp.sum(earlier.astype(jnp.int32), axis=1)
    place = jnp.where(live, owner * slots + ranks, -1)
    match = place[None, :] == index[:, None]
    taken = jnp.sum(match.astype(jnp.int32), axis=1)
    chosen = jnp.sum(jnp.where(match, index[None, :], 0), axis=1)
    free = jnp.sum(jnp.where(index[None, :] < index[:, None], 1 - taken[None, :], 0), axis=1)
    chosen = jnp.where(taken > 0, chosen, count + free)
    return jnp.sum(jnp.where(chosen[:, None] == index[None, :], accept[None, :], 0), axis=1)


def place_in_mesh():
    group, tensor = lax.axis_index("group"), lax.axis_index("tensor")
    return group // 2, group % 2, tensor // 4, (tensor // 2) % 2, tensor % 2


def device(z, low, y, high, core):
    return (z * 2 + low, y * 4 + high * 2 + core)


def enter(peers):
    barrier = pltpu.get_barrier_semaphore()
    for peer in peers:
        pl.semaphore_signal(barrier, inc=1, device_id=peer, device_id_type=MESH)
    pl.semaphore_wait(barrier, len(peers))


def send(src, dst, send_sem, recv_sem, peer):
    return pltpu.make_async_remote_copy(
        src_ref=src, dst_ref=dst, send_sem=send_sem, recv_sem=recv_sem,
        device_id=peer, device_id_type=MESH,
    )


class RingGather:
    def __init__(self, block, ring, pair, other, up, down, sends, recvs):
        self.block, self.ring, self.pair = block, ring, pair
        self.other, self.up, self.down = other, up, down
        self.sends, self.recvs = sends, recvs
        self.started = []

    def _go(self, src, dst, k, peer):
        copy = send(src, dst, self.sends.at[k], self.recvs.at[k], peer)
        copy.start()
        self.started.append(copy)

    def _arrived(self, ref, k, peer):
        send(ref, ref, self.sends.at[k], self.recvs.at[k], peer).wait_recv()

    def own(self, src):
        mine = self.block(self.ring, self.pair, None)
        self._go(src, mine, 1, self.up)
        self._go(src, mine, 2, self.down)
        self._go(src, mine, 0, self.other)

    def relay_pair(self):
        ref = self.block(self.ring, 1 - self.pair, None)
        self._arrived(ref, 0, self.other)
        self._go(ref, ref, 3, self.up)
        self._go(ref, ref, 4, self.down)
        return [ref]

    def relay_ring(self, flip):
        side = 1 - self.pair if flip else self.pair
        below, above = (self.ring + 3) % 4, (self.ring + 1) % 4
        k = 2 if flip else 0
        low, high = self.block(below, side, None), self.block(above, side, None)
        self._arrived(low, 1 + k, self.down)
        half = self.block(below, side, 0)
        self._go(half, half, 5 + k, self.up)
        self._arrived(high, 2 + k, self.up)
        half = self.block(above, side, 1)
        self._go(half, half, 6 + k, self.down)
        return [low, high]

    def last(self, flip):
        side = 1 - self.pair if flip else self.pair
        far = (self.ring + 2) % 4
        k = 2 if flip else 0
        first, second = self.block(far, side, 0), self.block(far, side, 1)
        self._arrived(first, 5 + k, self.down)
        self._arrived(second, 6 + k, self.up)
        return [first, second]

    def drain(self):
        for copy in self.started:
            copy.wait_send()


class ChipScatter:
    def __init__(self, acc, first, second, y, high, peers, partner, bufs, sends, recvs):
        self.acc, self.first, self.second = acc, first, second
        self.y, self.high, self.peers, self.partner = y, high, peers, partner
        self.ya, self.xb, self.xs, self.xa, self.bs, self.yb, self.own = bufs
        self.sends, self.recvs = sends, recvs
        self.copies = {}

    def _go(self, src, dst, k, peer):
        copy = send(src, dst, self.sends.at[k], self.recvs.at[k], peer)
        copy.start()
        self.copies[k] = copy

    def start(self):
        for d in (1, 2, 3):
            to = (self.y + d) % 4
            self._go(self.acc.at[to, :, self.first], self.ya.at[d - 1], d - 1, self.peers[d - 1])
        self._go(self.acc.at[:, 1 - self.high, self.second], self.xb, 3, self.partner)

    def middle(self):
        for d in (1, 2, 3):
            self.copies[d - 1].wait_recv()

        def along_y(side):
            total = self.acc[self.y, side, self.first].astype(jnp.float32)
            for d in (0, 1, 2):
                total += self.ya[d, side].astype(jnp.float32)
            return total

        self.xs[...] = along_y(1 - self.high).astype(jnp.bfloat16)
        self._go(self.xs, self.xa, 4, self.partner)
        self.own[0] = along_y(self.high)
        self.copies[3].wait_recv()
        for d in (1, 2, 3):
            to = (self.y + d) % 4
            pair = self.acc[to, self.high, self.second].astype(jnp.float32) + self.xb[to].astype(jnp.float32)
            self.bs[d - 1] = pair.astype(jnp.bfloat16)
            self._go(self.bs.at[d - 1], self.yb.at[d - 1], 4 + d, self.peers[d - 1])
        self.own[1] = self.acc[self.y, self.high, self.second].astype(jnp.float32) + self.xb[self.y].astype(jnp.float32)

    def finish(self):
        self.copies[4].wait_recv()
        first = self.own[0] + self.xa[...].astype(jnp.float32)
        total = self.own[1]
        for d in (1, 2, 3):
            self.copies[4 + d].wait_recv()
            total += self.yb[d - 1].astype(jnp.float32)
        return first, total

    def drain(self):
        for copy in self.copies.values():
            copy.wait_send()


def scatter_buffers(rows, columns):
    return [
        pltpu.VMEM((3, 2, rows, columns), jnp.bfloat16),
        pltpu.VMEM((4, rows, columns), jnp.bfloat16),
        pltpu.VMEM((rows, columns), jnp.bfloat16),
        pltpu.VMEM((rows, columns), jnp.bfloat16),
        pltpu.VMEM((3, rows, columns), jnp.bfloat16),
        pltpu.VMEM((3, rows, columns), jnp.bfloat16),
        pltpu.VMEM((2, rows, columns), jnp.float32),
        pltpu.SemaphoreType.DMA((8,)),
        pltpu.SemaphoreType.DMA((8,)),
    ]


def join_kernel(
    rowp_ref, low_ref, mid_ref, res_ref, att_ref, w_ref,
    top_ref, gath_ref,
    wbuf, psend, prec, acc, lmbuf, topbuf, attp, resp,
    a0, a1, a2, a3, a4, a5, a6, as_, ar_,
    b0, b1, b2, b3, b4, b5, b6, bs_, br_,
    wsem, psem, qsem, gsend, grecv, hsend, hrecv, lsem,
):
    z, xl, y, xh, c = place_in_mesh()
    g = z * 2 + xl
    n_rows = att_ref.shape[0]
    half = n_rows // 2
    width = att_ref.shape[1]
    quarter = half // 2
    loads = [
        pltpu.make_async_copy(w_ref.at[:, pl.ds(k * width, width)], wbuf.at[k], wsem.at[k]) for k in range(16)
    ]
    for load in loads:
        load.start()
    sib = device(z, xl, y, xh, 1 - c)
    partner = device(z, xl, y, 1 - xh, c)
    peers = [device(z, xl, (y + d) % 4, xh, c) for d in (1, 2, 3)]
    other = device(z, 1 - xl, y, xh, c)
    up, down = device((z + 1) % 4, xl, y, xh, c), device((z + 3) % 4, xl, y, xh, c)
    enter([sib, partner, *peers, other, up, down])

    def gather(first, size, sends, recvs):
        def block(r, s, part):
            owners = pl.ds(0, 8) if part is None else pl.ds(part * 4, 4)
            return gath_ref.at[owners, r * 2 + s, :, pl.ds(first, size)]
        return RingGather(block, z, xl, other, up, down, sends, recvs)

    pick = (rowp_ref[...] == lax.broadcasted_iota(jnp.int32, (n_rows, n_rows), 1)).astype(jnp.bfloat16)

    def picked(ref, rows):
        return jnp.dot(pick[:rows], ref[...], preferred_element_type=jnp.float32)

    lmbuf[:, :, :width] = picked(low_ref, half).astype(jnp.bfloat16).reshape(8, half // 8, width)
    lmbuf[:, :, width:] = picked(mid_ref, half).astype(jnp.bfloat16).reshape(8, half // 8, width)
    lm = gather(0, 2 * width, gsend, grecv)
    lm.own(lmbuf)
    keep_lm = pltpu.make_async_copy(lmbuf, gath_ref.at[:, g, :, pl.ds(0, 2 * width)], lsem.at[0])
    keep_lm.start()
    attp[...] = picked(att_ref, n_rows).astype(jnp.bfloat16)
    for load in loads:
        load.wait()

    def to_sibling(r, b):
        rows = pl.ds(r * half, half)
        return send(psend.at[b, rows], prec.at[b, rows], psem.at[r, b], qsem.at[r, b], sib)

    def product(r):
        rows = pl.ds(r * half, half)

        def theirs(b, _):
            part = jnp.dot(attp[rows], wbuf[2 * b + 1 - c], preferred_element_type=jnp.float32)
            psend[b, rows] = part.astype(jnp.bfloat16)
            to_sibling(r, b).start()
            return 0

        lax.fori_loop(0, 8, theirs, 0)

        def ours(b, _):
            part = jnp.dot(attp[rows], wbuf[2 * b + c], preferred_element_type=jnp.float32)
            to_sibling(r, b).wait_recv()
            acc[b // 2, b % 2, rows] = (part + prec[b, rows].astype(jnp.float32)).astype(jnp.bfloat16)
            return 0

        lax.fori_loop(0, 8, ours, 0)

    def scatter(r, bufs, sends, recvs):
        return ChipScatter(
            acc, pl.ds(r * half, quarter), pl.ds(r * half + quarter, quarter), y, xh, peers, partner, bufs, sends, recvs
        )

    product(0)
    rs0 = scatter(0, (a0, a1, a2, a3, a4, a5, a6), as_, ar_)
    rs0.start()
    lm.relay_pair()
    product(1)
    resp[...] = picked(res_ref, n_rows)
    rs0.middle()
    lm.relay_ring(False)
    first, second = rs0.finish()
    first = (resp[:quarter] + first).astype(jnp.bfloat16)
    second = (resp[quarter:half] + second).astype(jnp.bfloat16)
    topbuf[:4] = first.reshape(4, half // 8, width)
    topbuf[4:] = second.reshape(4, half // 8, width)
    top = gather(2 * width, width, hsend, hrecv)
    top.own(topbuf)
    keep_top = pltpu.make_async_copy(topbuf, gath_ref.at[:, g, :, pl.ds(2 * width, width)], lsem.at[1])
    keep_top.start()
    rs1 = scatter(1, (b0, b1, b2, b3, b4, b5, b6), bs_, br_)
    rs1.start()
    top_ref[:quarter] = first
    top_ref[quarter:half] = second
    lm.relay_ring(True)
    top.relay_pair()
    rs1.middle()
    top.relay_ring(False)
    top.relay_ring(True)
    first, second = rs1.finish()
    top_ref[half:half + quarter] = (resp[half:half + quarter] + first).astype(jnp.bfloat16)
    top_ref[half + quarter:] = (resp[half + quarter:] + second).astype(jnp.bfloat16)
    for flip in (False, True):
        lm.last(flip)
        top.last(flip)

    def sent(b, _):
        to_sibling(0, b).wait_send()
        to_sibling(1, b).wait_send()
        return 0

    lax.fori_loop(0, 8, sent, 0)
    for part in (lm, top, rs0, rs1):
        part.drain()
    keep_lm.wait()
    keep_top.wait()


def back_kernel(
    x_ref, w_ref, target_ref, gain_ref, weight_ref,
    back_ref,
    psend, prec, acc, stat, stats, own_back,
    a0, a1, a2, a3, a4, a5, a6, as_, ar_,
    psem, qsem, ssend, srecv, gsend, grecv, dsend, drecv, lsem,
):
    z, xl, y, xh, c = place_in_mesh()
    g = z * 2 + xl
    tensor = lax.axis_index("tensor")
    sib = device(z, xl, y, xh, 1 - c)
    partner = device(z, xl, y, 1 - xh, c)
    peers = [device(z, xl, (y + d) % 4, xh, c) for d in (1, 2, 3)]
    replicas = [((g + d) % 8, tensor) for d in range(1, 8)]
    enter([sib, partner, *peers, *replicas])
    features = x_ref.shape[3]
    columns = w_ref.shape[1]
    share = target_ref.shape[0]
    step = columns // 4

    def to_sibling(n):
        return send(psend.at[n], prec.at[n], psem.at[n], qsem.at[n], sib)

    def part(core, n):
        rows = x_ref[:, pl.ds(core * 4, 4)].reshape(8 * share, features)
        return jnp.dot(rows, w_ref[:, pl.ds(pl.multiple_of(n * step, step), step)], preferred_element_type=jnp.float32)

    def theirs(n, _):
        psend[n] = part(1 - c, n).astype(jnp.bfloat16)
        to_sibling(n).start()
        return 0

    lax.fori_loop(0, 4, theirs, 0)

    def ours(n, _):
        mine = part(c, n)
        to_sibling(n).wait_recv()
        both = (mine + prec[n].astype(jnp.float32)).astype(jnp.bfloat16)
        acc[:, :, :, pl.ds(pl.multiple_of(n * step, step), step)] = both.reshape(4, 2, share, step)
        return 0

    lax.fori_loop(0, 4, ours, 0)
    rs = ChipScatter(
        acc, pl.ds(0, share // 2), pl.ds(share // 2, share // 2), y, xh, peers, partner,
        (a0, a1, a2, a3, a4, a5, a6), as_, ar_,
    )
    rs.start()
    rs.middle()
    first, second = rs.finish()
    combined = jnp.concatenate([first, second], axis=0)
    gain = gain_ref[...]
    target = target_ref[...].astype(jnp.float32)
    gained = combined * gain
    lane = lax.broadcasted_iota(jnp.int32, (share, 128), 1)
    sums = jnp.where(
        lane == 0, jnp.sum(combined * combined, axis=1, keepdims=True),
        jnp.where(
            lane == 1, jnp.sum(gained * gained, axis=1, keepdims=True),
            jnp.sum(gained * target, axis=1, keepdims=True),
        ),
    )
    stat[...] = sums.T[:8]
    copies = [
        send(stat, stats.at[d - 1], ssend.at[d - 1], srecv.at[d - 1], replicas[d - 1]) for d in range(1, 8)
    ]
    for copy in copies:
        copy.start()
    total = stat[...]
    for d in range(7):
        copies[d].wait_recv()
        total += stats[d]
    total = jnp.concatenate([total, jnp.zeros((120, share), jnp.float32)], axis=0).T
    scale = lax.rsqrt(total[:, 0:1] / D + epsilon)
    weight = weight_ref[...]
    inner = weight * (scale * total[:, 1:2] - total[:, 2:3])
    slope = weight * (gained * scale - target)
    back = scale * gain * slope - combined * (scale * scale * scale * inner / D)
    own_back[...] = back.astype(jnp.bfloat16)

    def block(r, s, half):
        if half is None:
            return back_ref.at[r * 2 + s, c]
        return back_ref.at[r * 2 + s, c, pl.ds(half * (share // 2), share // 2)]

    ag = RingGather(block, y, xh, partner, peers[0], peers[2], gsend, grecv)
    ag.own(own_back)
    keep = pltpu.make_async_copy(own_back, back_ref.at[y * 2 + xh, c], lsem.at[0])
    keep.start()
    over = []

    def across(k, src, ref):
        copy = send(src, ref, dsend.at[k], drecv.at[k], sib)
        copy.start()
        over.append(copy)

    across(0, own_back, block(y, xh, None))
    across(1, *ag.relay_pair() * 2)
    k = 2
    for flip in (False, True):
        for ref in ag.relay_ring(flip):
            across(k, ref, ref)
            k += 1
    for flip in (False, True):
        for ref in ag.last(flip):
            across(k, ref, ref)
            k += 1

    def theirs_at(r, s, half):
        if half is None:
            return back_ref.at[r * 2 + s, 1 - c]
        return back_ref.at[r * 2 + s, 1 - c, pl.ds(half * (share // 2), share // 2)]

    below, above, far = (y + 3) % 4, (y + 1) % 4, (y + 2) % 4
    landed = [
        (y, xh, None), (y, 1 - xh, None),
        (below, xh, None), (above, xh, None), (below, 1 - xh, None), (above, 1 - xh, None),
        (far, xh, 0), (far, xh, 1), (far, 1 - xh, 0), (far, 1 - xh, 1),
    ]
    for k, at in enumerate(landed):
        ref = theirs_at(*at)
        send(ref, ref, dsend.at[k], drecv.at[k], sib).wait_recv()
    for copy in (*copies, *over):
        copy.wait_send()

    def sent(n, _):
        to_sibling(n).wait_send()
        return 0

    lax.fori_loop(0, 4, sent, 0)
    rs.drain()
    ag.drain()
    keep.wait()


def shards(
    low_state, mid_state, residual, attention, o_weight, fc_weight, norm_gain, target, counts, accept_rows, owners,
):
    group_count = lax.axis_size("group")
    group_index = lax.axis_index("group")
    tensor_index = lax.axis_index("tensor")
    rows, width = attention.shape
    half, quarter = rows // 2, rows // 4
    slots = half // group_count
    rowp = row_plan(counts, accept_rows, owners, group_count, group_index, slots)
    vmem = pl.BlockSpec(memory_space=pltpu.VMEM)
    anywhere = pl.BlockSpec(memory_space=pl.ANY)
    dma = pltpu.SemaphoreType.DMA
    bf16 = jnp.bfloat16
    top_perm, gathered = pl.pallas_call(
        join_kernel,
        out_shape=(
            jax.ShapeDtypeStruct((rows, width), bf16),
            jax.ShapeDtypeStruct((8, 8, slots, 3 * width), bf16),
        ),
        in_specs=[vmem, vmem, vmem, vmem, vmem, anywhere],
        out_specs=(vmem, anywhere),
        scratch_shapes=[
            pltpu.VMEM((16, width, width), bf16),
            pltpu.VMEM((8, rows, width), bf16),
            pltpu.VMEM((8, rows, width), bf16),
            pltpu.VMEM((4, 2, rows, width), bf16),
            pltpu.VMEM((8, slots, 2 * width), bf16),
            pltpu.VMEM((8, slots, width), bf16),
            pltpu.VMEM((rows, width), bf16),
            pltpu.VMEM((rows, width), jnp.float32),
            *scatter_buffers(quarter, width),
            *scatter_buffers(quarter, width),
            dma((16,)), dma((2, 8)), dma((2, 8)), dma((9,)), dma((9,)), dma((9,)), dma((9,)), dma((2,)),
        ],
        compiler_params=pltpu.CompilerParams(collective_id=0, has_side_effects=True, vmem_limit_bytes=48 << 20),
        cost_estimate=pl.CostEstimate(flops=2 * rows * width * D, bytes_accessed=16 << 20, transcendentals=0),
    )(rowp[:, None], low_state, mid_state, residual, attention, o_weight)

    share, columns = target.shape
    owner = tensor_index // 2
    first = (tensor_index % 2) * 4
    mine_owners = lax.dynamic_slice_in_dim(owners, first, 4, 0)
    mine_counts = lax.dynamic_slice_in_dim(counts, first, 4, 0)
    pairs = jnp.sum(
        ((mine_owners == owner) & (jnp.arange(rows, dtype=jnp.int32)[None, :] < mine_counts[:, None])).astype(jnp.int32),
        axis=1,
    )
    valid = (jnp.arange(slots, dtype=jnp.int32)[None, :] < pairs[:, None]).astype(jnp.float32)
    weight = valid.reshape(share, 1) / jnp.sum(counts).astype(jnp.float32)
    weights = fc_weight.reshape(3 * width, columns)
    back = pl.pallas_call(
        back_kernel,
        out_shape=jax.ShapeDtypeStruct((8, 2, share, columns), bf16),
        in_specs=[vmem] * 5,
        out_specs=anywhere,
        scratch_shapes=[
            pltpu.VMEM((4, 8 * share, columns // 4), bf16),
            pltpu.VMEM((4, 8 * share, columns // 4), bf16),
            pltpu.VMEM((4, 2, share, columns), bf16),
            pltpu.VMEM((8, share), jnp.float32),
            pltpu.VMEM((7, 8, share), jnp.float32),
            pltpu.VMEM((share, columns), bf16),
            *scatter_buffers(share // 2, columns),
            dma((4,)), dma((4,)), dma((7,)), dma((7,)), dma((9,)), dma((9,)), dma((10,)), dma((10,)), dma((1,)),
        ],
        compiler_params=pltpu.CompilerParams(collective_id=1, has_side_effects=True, vmem_limit_bytes=48 << 20),
        cost_estimate=pl.CostEstimate(flops=4 * rows * 12 * width * columns, bytes_accessed=16 << 20, transcendentals=0),
    )(gathered, weights, target, norm_gain[None, :], weight)
    grad = lax.dot_general(
        gathered.reshape(16 * share, 3 * width),
        back.reshape(16 * share, columns),
        (((0,), (0,)), ((), ())),
        preferred_element_type=jnp.float32,
    )
    put = (rowp[:, None] == jnp.arange(rows, dtype=jnp.int32)[None, :]).astype(bf16)
    top_state = lax.dot_general(
        put, top_perm, (((0,), (0,)), ((), ())), preferred_element_type=jnp.float32
    ).astype(bf16)
    return (top_state, grad.reshape(fc_weight.shape))


def solution(mesh):
    in_specs = (
        P("group", "tensor"),
        P("group", "tensor"),
        P("group", "tensor"),
        P("group", "tensor"),
        P("tensor", None),
        P(None, "tensor", "group"),
        P("group"),
        P("tensor", "group"),
        P(),
        P(),
        P(),
    )
    out_specs = (P("group", "tensor"), P(None, "tensor", "group"))
    return jax.shard_map(shards, mesh=mesh, in_specs=in_specs, out_specs=out_specs, check_vma=False)
```

```python
import jax
import jax.numpy as jnp
from jax import lax
from jax.experimental import pallas as pl
from jax.experimental.pallas import tpu as pltpu
from jax.sharding import PartitionSpec as P

D = 8192
SLOTS = 32
MESH = pl.DeviceIdType.MESH

epsilon = 1e-05


def place_in_mesh():
    group, tensor = lax.axis_index("group"), lax.axis_index("tensor")
    return group // 2, group % 2, tensor // 4, (tensor // 2) % 2, tensor % 2


def device(z, low, y, high, core):
    return (z * 2 + low, y * 4 + high * 2 + core)


def enter(peers):
    barrier = pltpu.get_barrier_semaphore()
    for peer in peers:
        pl.semaphore_signal(barrier, inc=1, device_id=peer, device_id_type=MESH)
    pl.semaphore_wait(barrier, len(peers))


def send(src, dst, send_sem, recv_sem, peer):
    return pltpu.make_async_remote_copy(
        src_ref=src, dst_ref=dst, send_sem=send_sem, recv_sem=recv_sem,
        device_id=peer, device_id_type=MESH,
    )


class RingGather:
    def __init__(self, block, other, up, down, sends, recvs):
        self.block, self.other, self.up, self.down = block, other, up, down
        self.sends, self.recvs = sends, recvs
        self.started = []

    def _go(self, at, k, peer, view):
        copy = send(self.block(*at, (0, 0)), self.block(*at, view), self.sends.at[k], self.recvs.at[k], peer)
        copy.start()
        self.started.append(copy)

    def _arrived(self, at, k, peer):
        ref = self.block(*at, (0, 0))
        send(ref, ref, self.sends.at[k], self.recvs.at[k], peer).wait_recv()
        return ref

    def own(self):
        self._go((0, 0, None), 1, self.up, (1, 0))
        self._go((0, 0, None), 2, self.down, (3, 0))
        self._go((0, 0, None), 0, self.other, (0, 1))

    def relay_pair(self):
        ref = self._arrived((0, 1, None), 0, self.other)
        self._go((0, 1, None), 3, self.up, (1, 0))
        self._go((0, 1, None), 4, self.down, (3, 0))
        return [ref]

    def relay_ring(self, flip):
        k = 2 * flip
        low = self._arrived((3, flip, None), 1 + k, self.down)
        self._go((3, flip, 0), 5 + k, self.up, (1, 0))
        high = self._arrived((1, flip, None), 2 + k, self.up)
        self._go((1, flip, 1), 6 + k, self.down, (3, 0))
        return [low, high]

    def last(self, flip):
        k = 2 * flip
        first = self._arrived((2, flip, 0), 5 + k, self.down)
        second = self._arrived((2, flip, 1), 6 + k, self.up)
        return [first, second]

    def drain(self):
        for copy in self.started:
            copy.wait_send()


class ChipScatter:
    def __init__(self, acc, first, second, y, high, peers, partner, bufs, sends, recvs):
        self.acc, self.first, self.second = acc, first, second
        self.y, self.high, self.peers, self.partner = y, high, peers, partner
        self.ya, self.xb, self.xs, self.xa, self.bs, self.yb, self.own = bufs
        self.sends, self.recvs = sends, recvs
        self.copies = {}

    def _go(self, src, dst, k, peer):
        copy = send(src, dst, self.sends.at[k], self.recvs.at[k], peer)
        copy.start()
        self.copies[k] = copy

    def start(self):
        for d in (1, 2, 3):
            to = (self.y + d) % 4
            self._go(self.acc.at[to, :, self.first], self.ya.at[d - 1], d - 1, self.peers[d - 1])
        self._go(self.acc.at[:, 1 - self.high, self.second], self.xb, 3, self.partner)

    def middle(self):
        for d in (1, 2, 3):
            self.copies[d - 1].wait_recv()

        def along_y(side):
            total = self.acc[self.y, side, self.first].astype(jnp.float32)
            for d in (0, 1, 2):
                total += self.ya[d, side].astype(jnp.float32)
            return total

        self.xs[...] = along_y(1 - self.high).astype(jnp.bfloat16)
        self._go(self.xs, self.xa, 4, self.partner)
        self.own[0] = along_y(self.high)
        self.copies[3].wait_recv()
        for d in (1, 2, 3):
            to = (self.y + d) % 4
            pair = self.acc[to, self.high, self.second].astype(jnp.float32) + self.xb[to].astype(jnp.float32)
            self.bs[d - 1] = pair.astype(jnp.bfloat16)
            self._go(self.bs.at[d - 1], self.yb.at[d - 1], 4 + d, self.peers[d - 1])
        self.own[1] = self.acc[self.y, self.high, self.second].astype(jnp.float32) + self.xb[self.y].astype(jnp.float32)

    def finish(self):
        self.copies[4].wait_recv()
        first = self.own[0] + self.xa[...].astype(jnp.float32)
        total = self.own[1]
        for d in (1, 2, 3):
            self.copies[4 + d].wait_recv()
            total += self.yb[d - 1].astype(jnp.float32)
        return first, total

    def drain(self):
        for copy in self.copies.values():
            copy.wait_send()


def scatter_buffers(rows, columns):
    return [
        pltpu.VMEM((3, 2, rows, columns), jnp.bfloat16),
        pltpu.VMEM((4, rows, columns), jnp.bfloat16),
        pltpu.VMEM((rows, columns), jnp.bfloat16),
        pltpu.VMEM((rows, columns), jnp.bfloat16),
        pltpu.VMEM((3, rows, columns), jnp.bfloat16),
        pltpu.VMEM((3, rows, columns), jnp.bfloat16),
        pltpu.VMEM((2, rows, columns), jnp.float32),
        pltpu.SemaphoreType.DMA((8,)),
        pltpu.SemaphoreType.DMA((8,)),
    ]


def group_block(ref, rows):
    order = {0: 0, 1: 1, 3: 2, 2: 3}

    def block(r, s, half, view):
        slot = order[(r - view[0]) % 4] * 2 + (s ^ view[1])
        if half is None:
            return ref.at[slot]
        return ref.at[slot, pl.ds(half * (rows // 2), rows // 2)]

    return block


def step_kernel(
    counts_ref, owners_ref, accept_ref, gain_ref, low_hbm, mid_hbm, res_hbm, att_hbm, w_hbm, fc_hbm, target_hbm,
    top_ref, xct_ref, back_ref,
    low, mid, res, att, wbuf, fcw, target,
    psend, prec, acc, gl, gt, attp, resp, ylm, topacc, hits, ranks,
    tsend, trecv, tacc, dsend, drecv, dacc, stat, stats, own_back,
    a0, a1, a2, a3, a4, a5, a6, as_, ar_,
    b0, b1, b2, b3, b4, b5, b6, bs_, br_,
    c0, c1, c2, c3, c4, c5, c6, cs_, cr_,
    d0, d1, d2, d3, d4, d5, d6, ds_, dr_,
    lsem, wsem, psem, qsem, gsend, grecv, hsend, hrecv, tsem, usem, esem, fsem, ssend, srecv, isend, irecv, jsend, jrecv,
    xsem, ksem,
):
    z, xl, y, xh, c = place_in_mesh()
    g, tensor = lax.axis_index("group"), lax.axis_index("tensor")
    bf16, f32 = jnp.bfloat16, jnp.float32
    n_rows, width = att.shape
    half = n_rows // 2
    quarter = half // 2
    columns = fcw.shape[1]
    share = own_back.shape[0]
    compact = 16 * share
    mine_half = compact // 2

    small = [
        pltpu.make_async_copy(src, dst, lsem.at[k])
        for k, (src, dst) in enumerate(
            ((low_hbm, low), (mid_hbm, mid), (att_hbm, att), (res_hbm, res), (target_hbm, target), (fc_hbm, fcw))
        )
    ]
    loads = [
        pltpu.make_async_copy(
            w_hbm.at[:, pl.ds(k * width, width)], wbuf.at[:, pl.ds(k * width, width)], wsem.at[k]
        )
        for k in range(16)
    ]
    for load in (*small[:3], *loads, *small[3:]):
        load.start()
    sib = device(z, xl, y, xh, 1 - c)
    partner = device(z, xl, y, 1 - xh, c)
    peers = [device(z, xl, (y + d) % 4, xh, c) for d in (1, 2, 3)]
    other = device(z, 1 - xl, y, xh, c)
    up, down = device((z + 1) % 4, xl, y, xh, c), device((z + 3) % 4, xl, y, xh, c)
    replicas = [((g + d) % 8, tensor) for d in range(1, 8)]
    enter([sib, partner, *peers, *replicas])

    lane8 = lax.broadcasted_iota(jnp.int32, (n_rows, 8), 1)
    order = accept_ref[...].astype(f32).T
    order = jnp.sum(jnp.where(lane8 == g, order, 0.0), axis=1, keepdims=True).astype(jnp.int32)
    pick = (order == lax.broadcasted_iota(jnp.int32, (n_rows, n_rows), 1)).astype(bf16)

    def picked(ref, rows):
        return jnp.dot(pick[:rows], ref[...], preferred_element_type=f32)

    small[0].wait()
    gl[0, :, :width] = picked(low, half).astype(bf16)
    small[1].wait()
    gl[0, :, width:] = picked(mid, half).astype(bf16)
    lm = RingGather(group_block(gl, half), other, up, down, gsend, grecv)
    top = RingGather(group_block(gt, half), other, up, down, hsend, hrecv)
    lm.own()
    small[2].wait()
    attp[...] = picked(att, n_rows).astype(bf16)
    for load in loads:
        load.wait()

    def to_sibling(r, b):
        rows = pl.ds(r * half, half)
        return send(psend.at[b, rows], prec.at[b, rows], psem.at[r, b], qsem.at[r, b], sib)

    def weight(k):
        return wbuf[:, pl.ds(pl.multiple_of(k * width, width), width)]

    def product(r):
        rows = pl.ds(r * half, half)

        def theirs(b, _):
            part = jnp.dot(attp[rows], weight(2 * b + 1 - c), preferred_element_type=f32)
            psend[b, rows] = part.astype(bf16)
            to_sibling(r, b).start()
            return 0

        lax.fori_loop(0, 8, theirs, 0)

        def ours(b, _):
            part = jnp.dot(attp[rows], weight(2 * b + c), preferred_element_type=f32)
            to_sibling(r, b).wait_recv()
            acc[b // 2, b % 2, rows] = (part + prec[b, rows].astype(f32)).astype(bf16)
            return 0

        lax.fori_loop(0, 8, ours, 0)

    def scatter(into, first, second, bufs, sends, recvs):
        return ChipScatter(into, first, second, y, xh, peers, partner, bufs, sends, recvs)

    product(0)
    rs0 = scatter(acc, pl.ds(0, quarter), pl.ds(quarter, quarter), (a0, a1, a2, a3, a4, a5, a6), as_, ar_)
    rs0.start()
    lm.relay_pair()
    product(1)

    owner = tensor // 2
    position = lax.broadcasted_iota(jnp.int32, (8, n_rows), 1)
    replica = lax.broadcasted_iota(jnp.int32, (8, n_rows), 0)
    limit = jnp.zeros((8, n_rows), jnp.int32)
    for k in range(8):
        limit = jnp.where(replica == k, counts_ref[k], limit)
    hit = jnp.where((owners_ref[...] == owner) & (position < limit), 1.0, 0.0).astype(f32)
    before = lax.broadcasted_iota(jnp.int32, (n_rows, n_rows), 0) < lax.broadcasted_iota(jnp.int32, (n_rows, n_rows), 1)
    hits[...] = hit
    ranks[...] = jnp.dot(hit.astype(bf16), before.astype(bf16), preferred_element_type=f32)

    def offset(which):
        total = jnp.int32(0)
        for k in range(8):
            total += jnp.where(k < which, counts_ref[k], 0)
        return total

    rows_of = []
    for k in range(4):
        which = (tensor % 2) * 4 + k
        member = lax.broadcasted_iota(jnp.int32, (SLOTS, n_rows), 0).astype(f32)
        row = (lax.broadcasted_iota(jnp.int32, (SLOTS, n_rows), 1) + offset(which) + 1).astype(f32)
        here = (ranks[pl.ds(which, 1), :] == member) & (hits[pl.ds(which, 1), :] > 0.5)
        rows_of.append(jnp.sum(jnp.where(here, row, 0.0), axis=1, keepdims=True))
    slot_row = jnp.concatenate(rows_of, axis=0).astype(jnp.int32) - 1
    spread = (slot_row == lax.broadcasted_iota(jnp.int32, (4 * SLOTS, compact), 1)).astype(f32).T.astype(bf16)
    small[4].wait()
    placed = jnp.dot(spread, target[...], preferred_element_type=f32).astype(bf16)
    tacc[...] = placed.reshape(2, 4, 2, share, columns)
    swap_target = send(tacc.at[1 - c], trecv, tsem.at[0], usem.at[0], sib)
    swap_target.start()

    small[3].wait()
    resp[...] = picked(res, n_rows)
    rs0.middle()
    lm.relay_ring(0)
    first, second = rs0.finish()
    first = (resp[:quarter] + first).astype(bf16)
    second = (resp[quarter:half] + second).astype(bf16)
    gt[0, :quarter] = first
    gt[0, quarter:] = second
    top.own()
    top_ref[:quarter] = first
    top_ref[quarter:half] = second
    swap_target.wait_recv()
    tsend[...] = (tacc[c].astype(f32) + trecv[...].astype(f32)).astype(bf16)
    rst = scatter(tsend, pl.ds(0, share // 2), pl.ds(share // 2, share // 2), (c0, c1, c2, c3, c4, c5, c6), cs_, cr_)
    rst.start()
    rs1 = scatter(
        acc, pl.ds(half, quarter), pl.ds(half + quarter, quarter), (b0, b1, b2, b3, b4, b5, b6), bs_, br_
    )
    lm.relay_ring(1)

    for slot in range(8):
        step = (0, 1, 3, 2)[slot // 2]
        which = ((z + step) % 4) * 2 + (xl ^ (slot % 2))
        count = counts_ref[which]
        start = offset(which)
        for part in range(2):
            column = lax.broadcasted_iota(jnp.int32, (mine_half, half), 1)
            row = lax.broadcasted_iota(jnp.int32, (mine_half, half), 0)
            hot = (row + (part * mine_half) - start == column) & (column < count)
            wbuf[:, pl.ds(part * 8 * half + slot * half, half)] = hot.astype(bf16)
    rst.middle()
    rs1.start()
    top.relay_pair()
    lm.last(0)
    lm.last(1)

    hot_width = 8 * half
    held = 2 * hot_width

    def compact_lm(part):
        hot = wbuf[:, pl.ds(part * hot_width, hot_width)]
        for chunk in range(2):
            rows = gl[:, :, chunk * width:(chunk + 1) * width].reshape(hot_width, width)
            got = jnp.dot(hot, rows, preferred_element_type=f32).astype(bf16)
            wbuf[:, pl.ds(held + part * 3 * width + chunk * width, width)] = got

    def product_lm(part):
        rows = wbuf[:, pl.ds(held + part * 3 * width, 2 * width)]
        for chunk in range(2):
            cols = pl.ds(chunk * width, width)
            ylm[part, :, cols] = jnp.dot(rows, fcw[:2 * width, cols], preferred_element_type=f32)

    def turned(part, chunk):
        block = wbuf[:, pl.ds(held + part * 3 * width + chunk * width, width)]
        psend[chunk * 2 + part] = block.T
        copy = pltpu.make_async_copy(
            psend.at[chunk * 2 + part],
            xct_ref.at[pl.ds(chunk * width, width), pl.ds(part * mine_half, mine_half)],
            xsem.at[chunk * 2 + part],
        )
        copy.start()
        return copy

    compact_lm(0)
    top.relay_ring(0)
    compact_lm(1)
    top.relay_ring(1)
    small[5].wait()
    product_lm(0)
    product_lm(1)
    first_t, second_t = rst.finish()
    rs1.middle()

    near = 6 * half

    def top_near(part):
        hot = wbuf[:, pl.ds(part * hot_width, near)]
        topacc[part] = jnp.dot(hot, gt[:6].reshape(near, width), preferred_element_type=f32)

    top_near(0)
    top_near(1)
    top.last(0)
    top.last(1)

    def top_part(part):
        hot = wbuf[:, pl.ds(pl.multiple_of(part * hot_width + near, half), 2 * half)]
        rows = topacc[part] + jnp.dot(hot, gt[6:].reshape(2 * half, width), preferred_element_type=f32)
        rows = rows.astype(bf16)
        wbuf[:, pl.ds(pl.multiple_of(held + part * 3 * width + 2 * width, width), width)] = rows
        return ylm[part] + jnp.dot(rows, fcw[2 * width:], preferred_element_type=f32)

    dsend[...] = top_part(1 - c).astype(bf16)
    swap = send(dsend, drecv, esem.at[0], fsem.at[0], sib)
    swap.start()
    mine = top_part(c)
    swap.wait_recv()
    dacc[...] = (mine + drecv[...].astype(f32)).astype(bf16).reshape(4, 2, share, columns)
    rs2 = scatter(dacc, pl.ds(0, share // 2), pl.ds(share // 2, share // 2), (d0, d1, d2, d3, d4, d5, d6), ds_, dr_)
    rs2.start()

    def sent(b, _):
        to_sibling(0, b).wait_send()
        to_sibling(1, b).wait_send()
        return 0

    lax.fori_loop(0, 8, sent, 0)
    rs2.middle()
    turns = [turned(part, chunk) for part in range(2) for chunk in range(3)]
    first, second = rs2.finish()

    combined = jnp.concatenate([first, second], axis=0)
    wanted = jnp.concatenate([first_t, second_t], axis=0)
    gain = gain_ref[...]
    gained = combined * gain
    lane = lax.broadcasted_iota(jnp.int32, (share, 128), 1)
    sums = jnp.where(
        lane == 0, jnp.sum(combined * combined, axis=1, keepdims=True),
        jnp.where(
            lane == 1, jnp.sum(gained * gained, axis=1, keepdims=True),
            jnp.sum(gained * wanted, axis=1, keepdims=True),
        ),
    )
    stat[...] = jnp.concatenate([sums, jnp.zeros((128 - share, 128), f32)], axis=0).T[:8]
    copies = [send(stat, stats.at[d - 1], ssend.at[d - 1], srecv.at[d - 1], replicas[d - 1]) for d in range(1, 8)]
    for copy in copies:
        copy.start()
    total = stat[...]
    for d in range(7):
        copies[d].wait_recv()
        total += stats[d]
    total = jnp.concatenate([total, jnp.zeros((120, 128), f32)], axis=0).T[:share]
    scale = lax.rsqrt(total[:, 0:1] / D + epsilon)
    weight = 1.0 / offset(8).astype(f32)
    inner = weight * (scale * total[:, 1:2] - total[:, 2:3])
    slope = weight * (gained * scale - wanted)
    own_back[...] = (scale * gain * slope - combined * (scale * scale * scale * inner / D)).astype(bf16)

    def back_at(r, s, part, core):
        chip = ((y + r) % 4) * 2 + (xh + s) % 2
        if part is None:
            return back_ref.at[core, chip]
        return back_ref.at[core, chip, pl.ds(part * (share // 2), share // 2)]

    def back_block(r, s, part, view):
        if (r, s) == (0, 0) and view == (0, 0):
            return own_back
        return back_at(r, s, part, c)

    ag = RingGather(back_block, partner, peers[0], peers[2], isend, irecv)
    ag.own()
    keep = pltpu.make_async_copy(own_back, back_at(0, 0, None, c), ksem.at[0])
    keep.start()
    over = []

    def across(src, ref):
        k = len(over)
        copy = send(src, ref, jsend.at[k], jrecv.at[k], sib)
        copy.start()
        over.append(copy)

    across(own_back, back_at(0, 0, None, c))
    for ref in ag.relay_pair():
        across(ref, ref)
    for flip in (0, 1):
        for ref in ag.relay_ring(flip):
            across(ref, ref)
    for flip in (0, 1):
        for ref in ag.last(flip):
            across(ref, ref)
    first, second = rs1.finish()
    top_ref[half:half + quarter] = (resp[half:half + quarter] + first).astype(bf16)
    top_ref[half + quarter:] = (resp[half + quarter:] + second).astype(bf16)
    landed = [
        (0, 0, None), (0, 1, None), (3, 0, None), (1, 0, None), (3, 1, None), (1, 1, None),
        (2, 0, 0), (2, 0, 1), (2, 1, 0), (2, 1, 1),
    ]
    for k, at in enumerate(landed):
        ref = back_at(*at, 1 - c)
        send(ref, ref, jsend.at[k], jrecv.at[k], sib).wait_recv()
    for copy in (*copies, *over, swap, swap_target):
        copy.wait_send()
    for part in (lm, top, ag, rs0, rs1, rst, rs2):
        part.drain()
    for copy in (*turns, keep):
        copy.wait()


def grad_kernel(accept_ref, top_ref, x_ref, back_ref, top_state_ref, grad_ref):
    g = lax.axis_index("group")
    rows = top_state_ref.shape[0]
    first = pl.program_id(0) * rows
    row = lax.broadcasted_iota(jnp.int32, (rows, top_ref.shape[0]), 0) + first
    put = (accept_ref[pl.ds(g, 1), :] == row).astype(jnp.bfloat16)
    top_state_ref[...] = jnp.dot(put, top_ref[...], preferred_element_type=jnp.float32).astype(jnp.bfloat16)
    grad_ref[...] = jnp.dot(x_ref[...], back_ref[...], preferred_element_type=jnp.float32)


def shards(
    low_state, mid_state, residual, attention, o_weight, fc_weight, norm_gain, target, counts, accept_rows, owners,
):
    rows, width = attention.shape
    half, quarter = rows // 2, rows // 4
    share, columns = target.shape[0] // 2, target.shape[1]
    compact = 16 * share
    vmem = pl.BlockSpec(memory_space=pltpu.VMEM)
    anywhere = pl.BlockSpec(memory_space=pl.ANY)
    dma = pltpu.SemaphoreType.DMA
    bf16, f32 = jnp.bfloat16, jnp.float32
    weights = fc_weight.reshape(3 * width, columns)
    top_perm, turned, back = pl.pallas_call(
        step_kernel,
        out_shape=(
            jax.ShapeDtypeStruct((rows, width), bf16),
            jax.ShapeDtypeStruct((3 * width, compact), bf16),
            jax.ShapeDtypeStruct((2, 8, share, columns), bf16),
        ),
        in_specs=[pl.BlockSpec(memory_space=pltpu.SMEM), vmem, vmem, vmem, *[anywhere] * 7],
        out_specs=(vmem, anywhere, anywhere),
        scratch_shapes=[
            pltpu.VMEM((rows, width), bf16),
            pltpu.VMEM((rows, width), bf16),
            pltpu.VMEM((rows, width), bf16),
            pltpu.VMEM((rows, width), bf16),
            pltpu.VMEM((width, D), bf16),
            pltpu.VMEM((3 * width, columns), bf16),
            pltpu.VMEM((2 * share, columns), bf16),
            pltpu.VMEM((8, rows, width), bf16),
            pltpu.VMEM((8, rows, width), bf16),
            pltpu.VMEM((4, 2, rows, width), bf16),
            pltpu.VMEM((8, half, 2 * width), bf16),
            pltpu.VMEM((8, half, width), bf16),
            pltpu.VMEM((rows, width), bf16),
            pltpu.VMEM((rows, width), f32),
            pltpu.VMEM((2, compact // 2, columns), f32),
            pltpu.VMEM((2, compact // 2, width), f32),
            pltpu.VMEM((8, rows), f32),
            pltpu.VMEM((8, rows), f32),
            pltpu.VMEM((4, 2, share, columns), bf16),
            pltpu.VMEM((4, 2, share, columns), bf16),
            pltpu.VMEM((2, 4, 2, share, columns), bf16),
            pltpu.VMEM((compact // 2, columns), bf16),
            pltpu.VMEM((compact // 2, columns), bf16),
            pltpu.VMEM((4, 2, share, columns), bf16),
            pltpu.VMEM((8, 128), f32),
            pltpu.VMEM((7, 8, 128), f32),
            pltpu.VMEM((share, columns), bf16),
            *scatter_buffers(quarter, width),
            *scatter_buffers(quarter, width),
            *scatter_buffers(share // 2, columns),
            *scatter_buffers(share // 2, columns),
            dma((6,)), dma((16,)), dma((2, 8)), dma((2, 8)), dma((9,)), dma((9,)), dma((9,)), dma((9,)),
            dma((1,)), dma((1,)), dma((1,)), dma((1,)), dma((7,)), dma((7,)), dma((9,)), dma((9,)), dma((10,)), dma((10,)),
            dma((6,)), dma((1,)),
        ],
        compiler_params=pltpu.CompilerParams(collective_id=0, has_side_effects=True, vmem_limit_bytes=62 << 20),
        cost_estimate=pl.CostEstimate(flops=2 * rows * width * D, bytes_accessed=16 << 20, transcendentals=0),
    )(counts, owners, accept_rows, norm_gain[None, :], low_state, mid_state, residual, attention, o_weight, weights, target)
    steps = 4
    top_state, grad = pl.pallas_call(
        grad_kernel,
        grid=(steps,),
        out_shape=(
            jax.ShapeDtypeStruct((rows, width), bf16),
            jax.ShapeDtypeStruct((3 * width, columns), f32),
        ),
        in_specs=[
            pl.BlockSpec((8, rows), lambda i: (0, 0)),
            pl.BlockSpec((rows, width), lambda i: (0, 0)),
            pl.BlockSpec((3 * width // steps, compact), lambda i: (i, 0)),
            pl.BlockSpec((compact, columns), lambda i: (0, 0)),
        ],
        out_specs=(
            pl.BlockSpec((rows // steps, width), lambda i: (i, 0)),
            pl.BlockSpec((3 * width // steps, columns), lambda i: (i, 0)),
        ),
        compiler_params=pltpu.CompilerParams(vmem_limit_bytes=40 << 20),
        cost_estimate=pl.CostEstimate(flops=6 * width * compact * columns, bytes_accessed=12 << 20, transcendentals=0),
    )(accept_rows, top_perm, turned, back.reshape(compact, columns))
    return (top_state, grad.reshape(fc_weight.shape))


def solution(mesh):
    in_specs = (
        P("group", "tensor"),
        P("group", "tensor"),
        P("group", "tensor"),
        P("group", "tensor"),
        P("tensor", None),
        P(None, "tensor", "group"),
        P("group"),
        P("tensor", "group"),
        P(),
        P(),
        P(),
    )
    out_specs = (P("group", "tensor"), P(None, "tensor", "group"))
    return jax.shard_map(shards, mesh=mesh, in_specs=in_specs, out_specs=out_specs, check_vma=False)
```

```python
import jax
import jax.numpy as jnp
from jax import lax
from jax.experimental import pallas as pl
from jax.experimental.pallas import tpu as pltpu
from jax.sharding import PartitionSpec as P

D = 8192
SLOTS = 32
MESH = pl.DeviceIdType.MESH

epsilon = 1e-05


def place_in_mesh():
    group, tensor = lax.axis_index("group"), lax.axis_index("tensor")
    return group // 2, group % 2, tensor // 4, (tensor // 2) % 2, tensor % 2


def device(z, low, y, high, core):
    return (z * 2 + low, y * 4 + high * 2 + core)


def enter(peers):
    barrier = pltpu.get_barrier_semaphore()
    for peer in peers:
        pl.semaphore_signal(barrier, inc=1, device_id=peer, device_id_type=MESH)
    pl.semaphore_wait(barrier, len(peers))


def send(src, dst, send_sem, recv_sem, peer):
    return pltpu.make_async_remote_copy(
        src_ref=src, dst_ref=dst, send_sem=send_sem, recv_sem=recv_sem,
        device_id=peer, device_id_type=MESH,
    )


class RingGather:
    def __init__(self, block, other, up, down, sends, recvs):
        self.block, self.other, self.up, self.down = block, other, up, down
        self.sends, self.recvs = sends, recvs
        self.started = []

    def _go(self, at, k, peer, view):
        copy = send(self.block(*at, (0, 0)), self.block(*at, view), self.sends.at[k], self.recvs.at[k], peer)
        copy.start()
        self.started.append(copy)

    def _arrived(self, at, k, peer):
        ref = self.block(*at, (0, 0))
        send(ref, ref, self.sends.at[k], self.recvs.at[k], peer).wait_recv()
        return ref

    def own(self):
        self._go((0, 0, None), 1, self.up, (1, 0))
        self._go((0, 0, None), 2, self.down, (3, 0))
        self._go((0, 0, None), 0, self.other, (0, 1))

    def relay_pair(self):
        ref = self._arrived((0, 1, None), 0, self.other)
        self._go((0, 1, None), 3, self.up, (1, 0))
        self._go((0, 1, None), 4, self.down, (3, 0))
        return [ref]

    def relay_ring(self, flip):
        k = 2 * flip
        low = self._arrived((3, flip, None), 1 + k, self.down)
        self._go((3, flip, 0), 5 + k, self.up, (1, 0))
        high = self._arrived((1, flip, None), 2 + k, self.up)
        self._go((1, flip, 1), 6 + k, self.down, (3, 0))
        return [low, high]

    def last(self, flip):
        k = 2 * flip
        first = self._arrived((2, flip, 0), 5 + k, self.down)
        second = self._arrived((2, flip, 1), 6 + k, self.up)
        return [first, second]

    def drain(self):
        for copy in self.started:
            copy.wait_send()


class ChipScatter:
    def __init__(self, acc, first, second, y, high, peers, partner, bufs, sends, recvs):
        self.acc, self.first, self.second = acc, first, second
        self.y, self.high, self.peers, self.partner = y, high, peers, partner
        self.ya, self.xb, self.xs, self.xa, self.bs, self.yb, self.own = bufs
        self.sends, self.recvs = sends, recvs
        self.copies = {}

    def _go(self, src, dst, k, peer):
        copy = send(src, dst, self.sends.at[k], self.recvs.at[k], peer)
        copy.start()
        self.copies[k] = copy

    def start(self):
        self.start_first()
        self.start_second()

    def start_first(self):
        for d in (1, 2, 3):
            to = (self.y + d) % 4
            self._go(self.acc.at[(to, slice(None), *self.first)], self.ya.at[d - 1], d - 1, self.peers[d - 1])

    def start_second(self):
        self._go(self.acc.at[(slice(None), 1 - self.high, *self.second)], self.xb, 3, self.partner)

    def middle(self):
        for d in (1, 2, 3):
            self.copies[d - 1].wait_recv()

        def along_y(side):
            total = self.acc[(self.y, side, *self.first)].astype(jnp.float32)
            for d in (0, 1, 2):
                total += self.ya[d, side].astype(jnp.float32)
            return total

        self.xs[...] = along_y(1 - self.high).astype(jnp.bfloat16)
        self._go(self.xs, self.xa, 4, self.partner)
        self.own[0] = along_y(self.high)
        self.copies[3].wait_recv()
        for d in (1, 2, 3):
            to = (self.y + d) % 4
            pair = self.acc[(to, self.high, *self.second)].astype(jnp.float32) + self.xb[to].astype(jnp.float32)
            self.bs[d - 1] = pair.astype(jnp.bfloat16)
            self._go(self.bs.at[d - 1], self.yb.at[d - 1], 4 + d, self.peers[d - 1])
        self.own[1] = self.acc[(self.y, self.high, *self.second)].astype(jnp.float32) + self.xb[self.y].astype(jnp.float32)

    def finish(self):
        self.copies[4].wait_recv()
        first = self.own[0] + self.xa[...].astype(jnp.float32)
        total = self.own[1]
        for d in (1, 2, 3):
            self.copies[4 + d].wait_recv()
            total += self.yb[d - 1].astype(jnp.float32)
        return first, total

    def drain(self):
        for copy in self.copies.values():
            copy.wait_send()


class RingScatter:
    def __init__(self, acc, halves, rest, y, high, peers, partner, bufs, sends, recvs):
        self.acc, self.halves, self.rest = acc, halves, rest
        self.y, self.high, self.peers, self.partner = y, high, peers, partner
        self.far, self.sums, self.below, self.above, self.xs, self.xa, self.own, self.xb, self.bs, self.yb, self.kept = bufs
        self.sends, self.recvs = sends, recvs
        self.copies = {}

    def _go(self, src, dst, k, peer):
        copy = send(src, dst, self.sends.at[k], self.recvs.at[k], peer)
        copy.start()
        self.copies[k] = copy

    def _block(self, step, side, half):
        return ((self.y + step) % 4, side, *self.halves[half])

    def start(self):
        both = slice(None)
        up, down = self.peers[0], self.peers[2]
        self._go(self.acc.at[self._block(2, both, 0)], self.far.at[0], 0, up)
        self._go(self.acc.at[self._block(2, both, 1)], self.far.at[1], 1, down)
        self._go(self.acc.at[(both, 1 - self.high, *self.rest)], self.xb, 4, self.partner)
        self._go(self.acc.at[self._block(1, both, 1)], self.below.at[1], 2, up)
        self._go(self.acc.at[self._block(3, both, 0)], self.above.at[0], 3, down)

    def relay(self):
        for half, step, into, peer in ((0, 1, self.below, self.peers[0]), (1, 3, self.above, self.peers[2])):
            self.copies[half].wait_recv()
            for side in (0, 1):
                total = self.acc[self._block(step, side, half)].astype(jnp.float32) + self.far[half, side].astype(jnp.float32)
                self.sums[half, side] = total.astype(jnp.bfloat16)
            self._go(self.sums.at[half], into.at[half], 5 + half, peer)
        self.copies[4].wait_recv()
        for d in (1, 2, 3):
            to = (self.y + d) % 4
            pair = self.acc[(to, self.high, *self.rest)].astype(jnp.float32) + self.xb[to].astype(jnp.float32)
            self.bs[d - 1] = pair.astype(jnp.bfloat16)
            self._go(self.bs.at[d - 1], self.yb.at[d - 1], 7 + d, self.peers[d - 1])
        self.kept[...] = self.acc[(self.y, self.high, *self.rest)].astype(jnp.float32) + self.xb[self.y].astype(jnp.float32)

    def middle(self):
        for k in (2, 3, 5, 6):
            self.copies[k].wait_recv()

        def along_y(side, half):
            total = self.acc[self._block(0, side, half)].astype(jnp.float32)
            return total + self.below[half, side].astype(jnp.float32) + self.above[half, side].astype(jnp.float32)

        for half in (0, 1):
            self.xs[half] = along_y(1 - self.high, half).astype(jnp.bfloat16)
        self._go(self.xs, self.xa, 7, self.partner)
        for half in (0, 1):
            self.own[half] = along_y(self.high, half)

    def finish(self):
        self.copies[7].wait_recv()
        rest = self.kept[...]
        for d in (1, 2, 3):
            self.copies[7 + d].wait_recv()
            rest += self.yb[d - 1].astype(jnp.float32)
        return self.own[0] + self.xa[0].astype(jnp.float32), self.own[1] + self.xa[1].astype(jnp.float32), rest

    def drain(self):
        for copy in self.copies.values():
            copy.wait_send()


def ring_buffers(half, rest):
    bf16, f32 = jnp.bfloat16, jnp.float32
    return [
        pltpu.VMEM((2, 2, *half), bf16),
        pltpu.VMEM((2, 2, *half), bf16),
        pltpu.VMEM((2, 2, *half), bf16),
        pltpu.VMEM((2, 2, *half), bf16),
        pltpu.VMEM((2, *half), bf16),
        pltpu.VMEM((2, *half), bf16),
        pltpu.VMEM((2, *half), f32),
        pltpu.VMEM((4, *rest), bf16),
        pltpu.VMEM((3, *rest), bf16),
        pltpu.VMEM((3, *rest), bf16),
        pltpu.VMEM(rest, f32),
        pltpu.SemaphoreType.DMA((11,)),
        pltpu.SemaphoreType.DMA((11,)),
    ]


def scatter_buffers(rows, columns):
    return [
        pltpu.VMEM((3, 2, rows, columns), jnp.bfloat16),
        pltpu.VMEM((4, rows, columns), jnp.bfloat16),
        pltpu.VMEM((rows, columns), jnp.bfloat16),
        pltpu.VMEM((rows, columns), jnp.bfloat16),
        pltpu.VMEM((3, rows, columns), jnp.bfloat16),
        pltpu.VMEM((3, rows, columns), jnp.bfloat16),
        pltpu.VMEM((2, rows, columns), jnp.float32),
        pltpu.SemaphoreType.DMA((8,)),
        pltpu.SemaphoreType.DMA((8,)),
    ]


def group_block(ref, rows):
    order = {0: 0, 1: 1, 3: 2, 2: 3}

    def block(r, s, half, view):
        slot = order[(r - view[0]) % 4] * 2 + (s ^ view[1])
        if half is None:
            return ref.at[slot]
        return ref.at[slot, pl.ds(half * (rows // 2), rows // 2)]

    return block


def step_kernel(
    counts_ref, owners_ref, accept_ref, gain_ref, low_hbm, mid_hbm, res_hbm, att_hbm, w_hbm, fc_hbm, target_hbm,
    top_ref, xct_ref, back_ref,
    low, mid, res, att, wbuf, fcw, target,
    psend, prec, acc, gl, gm, gt, attp, resp, ylm, topacc, hits, ranks,
    tsend, trecv, tacc, dsend, drecv, dacc, stat, stats, own_back, own_wanted,
    a0, a1, a2, a3, a4, a5, a6, a7, a8, a9, a10, as_, ar_,
    b0, b1, b2, b3, b4, b5, b6, b7, b8, b9, b10, bs_, br_,
    c0, c1, c2, c3, c4, c5, c6, c7, c8, c9, c10, cs_, cr_,
    d0, d1, d2, d3, d4, d5, d6, ds_, dr_,
    lsem, wsem, psem, qsem, gsend, grecv, msend, mrecv, hsend, hrecv, tsem, usem, esem, fsem, ssend, srecv, isend, irecv, jsend, jrecv,
    xsem, ksem,
):
    z, xl, y, xh, c = place_in_mesh()
    g, tensor = lax.axis_index("group"), lax.axis_index("tensor")
    bf16, f32 = jnp.bfloat16, jnp.float32
    n_rows, width = att.shape
    half = n_rows // 2
    columns = fcw.shape[1]
    share = own_back.shape[0]
    compact = 16 * share
    mine_half = compact // 2

    small = [
        pltpu.make_async_copy(src, dst, lsem.at[k])
        for k, (src, dst) in enumerate(
            ((low_hbm, low), (mid_hbm, mid), (att_hbm, att), (res_hbm, res), (target_hbm, target), (fc_hbm, fcw))
        )
    ]
    loads = [
        pltpu.make_async_copy(
            w_hbm.at[:, pl.ds(k * width, width)], wbuf.at[:, pl.ds(k * width, width)], wsem.at[k]
        )
        for k in range(16)
    ]
    for load in (*small[:3], *loads, *small[3:]):
        load.start()
    sib = device(z, xl, y, xh, 1 - c)
    partner = device(z, xl, y, 1 - xh, c)
    peers = [device(z, xl, (y + d) % 4, xh, c) for d in (1, 2, 3)]
    other = device(z, 1 - xl, y, xh, c)
    up, down = device((z + 1) % 4, xl, y, xh, c), device((z + 3) % 4, xl, y, xh, c)
    replicas = [((g + d) % 8, tensor) for d in range(1, 8)]
    enter([sib, partner, *peers, *replicas])

    lane8 = lax.broadcasted_iota(jnp.int32, (n_rows, 8), 1)
    order = accept_ref[...].astype(f32).T
    order = jnp.sum(jnp.where(lane8 == g, order, 0.0), axis=1, keepdims=True).astype(jnp.int32)
    pick = (order == lax.broadcasted_iota(jnp.int32, (n_rows, n_rows), 1)).astype(bf16)

    def picked(ref, rows):
        return jnp.dot(pick[:rows], ref[...], preferred_element_type=f32)

    low_part = RingGather(group_block(gl, half), other, up, down, gsend, grecv)
    mid_part = RingGather(group_block(gm, half), other, up, down, msend, mrecv)
    top = RingGather(group_block(gt, half), other, up, down, hsend, hrecv)
    small[0].wait()
    gl[0] = picked(low, half).astype(bf16)
    low_part.own()
    small[1].wait()
    gm[0] = picked(mid, half).astype(bf16)
    mid_part.own()
    small[2].wait()
    attp[...] = picked(att, n_rows).astype(bf16)
    for load in loads:
        load.wait()

    def to_sibling(r, b):
        rows = pl.ds(r * half, half)
        return send(psend.at[b, rows], prec.at[b, rows], psem.at[r, b], qsem.at[r, b], sib)

    def weight(k):
        return wbuf[:, pl.ds(pl.multiple_of(k * width, width), width)]

    def product(r):
        rows = pl.ds(r * half, half)

        def theirs(b, _):
            part = jnp.dot(attp[rows], weight(2 * b + 1 - c), preferred_element_type=f32)
            psend[b, rows] = part.astype(bf16)
            to_sibling(r, b).start()
            return 0

        lax.fori_loop(0, 8, theirs, 0)

        def ours(b, _):
            part = jnp.dot(attp[rows], weight(2 * b + c), preferred_element_type=f32)
            to_sibling(r, b).wait_recv()
            acc[b // 2, b % 2, rows] = (part + prec[b, rows].astype(f32)).astype(bf16)
            return 0

        lax.fori_loop(0, 8, ours, 0)

    cut = 3 * half // 8

    def scatter(into, halves, rest, bufs, sends, recvs):
        return RingScatter(into, halves, rest, y, xh, peers, partner, bufs, sends, recvs)

    def scatter_rows(r, bufs, sends, recvs):
        at = r * half
        return scatter(
            acc, ((pl.ds(at, cut),), (pl.ds(at + cut, cut),)), (pl.ds(at + 2 * cut, half - 2 * cut),), bufs, sends, recvs
        )

    def keep_top(r, sums):
        at = r * half
        for part in sums:
            rows = pl.ds(at, part.shape[0])
            top_ref[rows] = (resp[rows] + part).astype(bf16)
            at += part.shape[0]

    product(0)
    rs0 = scatter_rows(0, (a0, a1, a2, a3, a4, a5, a6, a7, a8, a9, a10), as_, ar_)
    rs0.start()
    low_part.relay_pair()
    product(1)
    mid_part.relay_pair()
    low_part.relay_ring(0)

    owner = tensor // 2
    position = lax.broadcasted_iota(jnp.int32, (8, n_rows), 1)
    replica = lax.broadcasted_iota(jnp.int32, (8, n_rows), 0)
    limit = jnp.zeros((8, n_rows), jnp.int32)
    for k in range(8):
        limit = jnp.where(replica == k, counts_ref[k], limit)
    hit = jnp.where((owners_ref[...] == owner) & (position < limit), 1.0, 0.0).astype(f32)
    before = lax.broadcasted_iota(jnp.int32, (n_rows, n_rows), 0) < lax.broadcasted_iota(jnp.int32, (n_rows, n_rows), 1)
    hits[...] = hit
    ranks[...] = jnp.dot(hit.astype(bf16), before.astype(bf16), preferred_element_type=f32)

    def offset(which):
        total = jnp.int32(0)
        for k in range(8):
            total += jnp.where(k < which, counts_ref[k], 0)
        return total

    rows_of = []
    for k in range(4):
        which = (tensor % 2) * 4 + k
        member = lax.broadcasted_iota(jnp.int32, (SLOTS, n_rows), 0).astype(f32)
        row = (lax.broadcasted_iota(jnp.int32, (SLOTS, n_rows), 1) + offset(which) + 1).astype(f32)
        here = (ranks[pl.ds(which, 1), :] == member) & (hits[pl.ds(which, 1), :] > 0.5)
        rows_of.append(jnp.sum(jnp.where(here, row, 0.0), axis=1, keepdims=True))
    slot_row = jnp.concatenate(rows_of, axis=0).astype(jnp.int32) - 1
    spread = (slot_row == lax.broadcasted_iota(jnp.int32, (4 * SLOTS, compact), 1)).astype(f32).T.astype(bf16)
    small[4].wait()
    placed = jnp.dot(spread, target[...], preferred_element_type=f32).astype(bf16)
    tacc[...] = placed.reshape(2, 4, 2, share, columns)
    swap_target = send(tacc.at[1 - c], trecv, tsem.at[0], usem.at[0], sib)
    swap_target.start()

    rs0.relay()
    low_part.relay_ring(1)
    mid_part.relay_ring(0)
    small[3].wait()
    resp[...] = picked(res, n_rows)

    def sent(b, _):
        to_sibling(0, b).wait_send()
        to_sibling(1, b).wait_send()
        return 0

    lax.fori_loop(0, 8, sent, 0)

    for slot in range(8):
        step = (0, 1, 3, 2)[slot // 2]
        which = ((z + step) % 4) * 2 + (xl ^ (slot % 2))
        count = counts_ref[which]
        start = offset(which)
        for part in range(2):
            column = lax.broadcasted_iota(jnp.int32, (mine_half, half), 1)
            row = lax.broadcasted_iota(jnp.int32, (mine_half, half), 0)
            hot = (row + (part * mine_half) - start == column) & (column < count)
            wbuf[:, pl.ds(part * 8 * half + slot * half, half)] = hot.astype(bf16)
    hot_width = 8 * half
    held = 2 * hot_width
    near = 6 * half

    def place(part, chunk):
        return pl.ds(held + part * 3 * width + chunk * width, width)

    def compact_rows(ref, chunk):
        for part in range(2):
            hot = wbuf[:, pl.ds(part * hot_width, hot_width)]
            rows = ref[...].reshape(hot_width, width)
            wbuf[:, place(part, chunk)] = jnp.dot(hot, rows, preferred_element_type=f32).astype(bf16)

    def product_rows(chunk):
        for part in range(2):
            for side in range(2):
                cols = pl.ds(side * width, width)
                got = jnp.dot(
                    wbuf[:, place(part, chunk)], fcw[chunk * width:(chunk + 1) * width, cols], preferred_element_type=f32
                )
                ylm[part, :, cols] = got if chunk == 0 else ylm[part, :, cols] + got

    turns = []

    def turn(chunk):
        for part in range(2):
            k = chunk * 2 + part
            psend[k] = wbuf[:, place(part, chunk)].T
            copy = pltpu.make_async_copy(
                psend.at[k],
                xct_ref.at[pl.ds(chunk * width, width), pl.ds(part * mine_half, mine_half)],
                xsem.at[k],
            )
            copy.start()
            turns.append(copy)

    rs0.middle()
    swap_target.wait_recv()
    tsend[...] = (tacc[c].astype(f32) + trecv[...].astype(f32)).astype(bf16)
    side = 3 * columns // 8
    every = pl.ds(0, share)
    rst = scatter(
        tsend, ((every, pl.ds(0, side)), (every, pl.ds(side, side))), (every, pl.ds(2 * side, columns - 2 * side)),
        (c0, c1, c2, c3, c4, c5, c6, c7, c8, c9, c10), cs_, cr_,
    )
    rst.start()
    mid_part.relay_ring(1)
    keep_top(0, rs0.finish())
    gt[0] = top_ref[:half]
    top.own()
    rs1 = scatter_rows(1, (b0, b1, b2, b3, b4, b5, b6, b7, b8, b9, b10), bs_, br_)
    rs1.start()
    low_part.last(0)
    low_part.last(1)
    compact_rows(gl, 0)
    rst.relay()
    small[5].wait()
    product_rows(0)
    rst.middle()
    top.relay_pair()
    rs1.relay()
    turn(0)
    mid_part.last(0)
    mid_part.last(1)
    compact_rows(gm, 1)
    top.relay_ring(0)
    product_rows(1)
    rs1.middle()
    own_wanted[...] = jnp.concatenate(rst.finish(), axis=1)
    turn(1)
    top.relay_ring(1)
    for part in range(2):
        hot = wbuf[:, pl.ds(part * hot_width, near)]
        topacc[part] = jnp.dot(hot, gt[:6].reshape(near, width), preferred_element_type=f32)
    top.last(0)
    top.last(1)

    def swap(side):
        return send(dsend.at[side], drecv.at[side], esem.at[side], fsem.at[side], sib)

    def top_rows(part):
        hot = wbuf[:, pl.ds(pl.multiple_of(part * hot_width + near, half), 2 * half)]
        rows = topacc[part] + jnp.dot(hot, gt[6:].reshape(2 * half, width), preferred_element_type=f32)
        rows = rows.astype(bf16)
        wbuf[:, pl.ds(pl.multiple_of(held + part * 3 * width + 2 * width, width), width)] = rows
        return rows

    def features(part, rows, side):
        cols = pl.ds(side * width, width)
        return ylm[part, :, cols] + jnp.dot(rows, fcw[2 * width:, cols], preferred_element_type=f32)

    rows = top_rows(1 - c)
    for side in range(2):
        dsend[side] = features(1 - c, rows, side).astype(bf16)
        swap(side).start()
    rs2 = ChipScatter(
        dacc, (slice(None), pl.ds(0, width)), (slice(None), pl.ds(width, width)), y, xh, peers, partner,
        (d0, d1, d2, d3, d4, d5, d6), ds_, dr_,
    )
    rows = top_rows(c)
    for side in range(2):
        mine = features(c, rows, side)
        swap(side).wait_recv()
        both = (mine + drecv[side].astype(f32)).astype(bf16)
        dacc[:, :, :, pl.ds(side * width, width)] = both.reshape(4, 2, share, width)
        if side == 0:
            rs2.start_first()
        else:
            rs2.start_second()
    rs2.middle()
    turn(2)
    first, second = rs2.finish()

    combined = jnp.concatenate([first, second], axis=1)
    wanted = own_wanted[...]
    gain = gain_ref[...]
    gained = combined * gain
    lane = lax.broadcasted_iota(jnp.int32, (share, 128), 1)
    sums = jnp.where(
        lane == 0, jnp.sum(combined * combined, axis=1, keepdims=True),
        jnp.where(
            lane == 1, jnp.sum(gained * gained, axis=1, keepdims=True),
            jnp.sum(gained * wanted, axis=1, keepdims=True),
        ),
    )
    stat[...] = jnp.concatenate([sums, jnp.zeros((128 - share, 128), f32)], axis=0).T[:8]
    copies = [send(stat, stats.at[d - 1], ssend.at[d - 1], srecv.at[d - 1], replicas[d - 1]) for d in range(1, 8)]
    for copy in copies:
        copy.start()
    total = stat[...]
    for d in range(7):
        copies[d].wait_recv()
        total += stats[d]
    total = jnp.concatenate([total, jnp.zeros((120, 128), f32)], axis=0).T[:share]
    scale = lax.rsqrt(total[:, 0:1] / D + epsilon)
    weight = 1.0 / offset(8).astype(f32)
    inner = weight * (scale * total[:, 1:2] - total[:, 2:3])
    slope = weight * (gained * scale - wanted)
    own_back[...] = (scale * gain * slope - combined * (scale * scale * scale * inner / D)).astype(bf16)

    def back_at(r, s, part, core):
        chip = ((y + r) % 4) * 2 + (xh + s) % 2
        if part is None:
            return back_ref.at[core, chip]
        return back_ref.at[core, chip, pl.ds(part * (share // 2), share // 2)]

    def back_block(r, s, part, view):
        if (r, s) == (0, 0) and view == (0, 0):
            return own_back
        return back_at(r, s, part, c)

    ag = RingGather(back_block, partner, peers[0], peers[2], isend, irecv)
    ag.own()
    keep = pltpu.make_async_copy(own_back, back_at(0, 0, None, c), ksem.at[0])
    keep.start()
    over = []

    def across(src, ref):
        k = len(over)
        copy = send(src, ref, jsend.at[k], jrecv.at[k], sib)
        copy.start()
        over.append(copy)

    across(own_back, back_at(0, 0, None, c))
    for ref in ag.relay_pair():
        across(ref, ref)
    for flip in (0, 1):
        for ref in ag.relay_ring(flip):
            across(ref, ref)
    for flip in (0, 1):
        for ref in ag.last(flip):
            across(ref, ref)
    keep_top(1, rs1.finish())
    landed = [
        (0, 0, None), (0, 1, None), (3, 0, None), (1, 0, None), (3, 1, None), (1, 1, None),
        (2, 0, 0), (2, 0, 1), (2, 1, 0), (2, 1, 1),
    ]
    for k, at in enumerate(landed):
        ref = back_at(*at, 1 - c)
        send(ref, ref, jsend.at[k], jrecv.at[k], sib).wait_recv()
    for copy in (*copies, *over, swap(0), swap(1), swap_target):
        copy.wait_send()
    for part in (low_part, mid_part, top, ag, rs0, rs1, rst, rs2):
        part.drain()
    for copy in (*turns, keep):
        copy.wait()


def grad_kernel(accept_ref, top_ref, x_ref, back_ref, top_state_ref, grad_ref):
    g = lax.axis_index("group")
    rows = top_state_ref.shape[0]
    first = pl.program_id(0) * rows
    row = lax.broadcasted_iota(jnp.int32, (rows, top_ref.shape[0]), 0) + first
    put = (accept_ref[pl.ds(g, 1), :] == row).astype(jnp.bfloat16)
    top_state_ref[...] = jnp.dot(put, top_ref[...], preferred_element_type=jnp.float32).astype(jnp.bfloat16)
    grad_ref[...] = jnp.dot(x_ref[...], back_ref[...], preferred_element_type=jnp.float32)


def shards(
    low_state, mid_state, residual, attention, o_weight, fc_weight, norm_gain, target, counts, accept_rows, owners,
):
    rows, width = attention.shape
    half = rows // 2
    share, columns = target.shape[0] // 2, target.shape[1]
    compact = 16 * share
    vmem = pl.BlockSpec(memory_space=pltpu.VMEM)
    anywhere = pl.BlockSpec(memory_space=pl.ANY)
    dma = pltpu.SemaphoreType.DMA
    bf16, f32 = jnp.bfloat16, jnp.float32
    weights = fc_weight.reshape(3 * width, columns)
    top_perm, turned, back = pl.pallas_call(
        step_kernel,
        out_shape=(
            jax.ShapeDtypeStruct((rows, width), bf16),
            jax.ShapeDtypeStruct((3 * width, compact), bf16),
            jax.ShapeDtypeStruct((2, 8, share, columns), bf16),
        ),
        in_specs=[pl.BlockSpec(memory_space=pltpu.SMEM), vmem, vmem, vmem, *[anywhere] * 7],
        out_specs=(vmem, anywhere, anywhere),
        scratch_shapes=[
            pltpu.VMEM((rows, width), bf16),
            pltpu.VMEM((rows, width), bf16),
            pltpu.VMEM((rows, width), bf16),
            pltpu.VMEM((rows, width), bf16),
            pltpu.VMEM((width, D), bf16),
            pltpu.VMEM((3 * width, columns), bf16),
            pltpu.VMEM((2 * share, columns), bf16),
            pltpu.VMEM((8, rows, width), bf16),
            pltpu.VMEM((8, rows, width), bf16),
            pltpu.VMEM((4, 2, rows, width), bf16),
            pltpu.VMEM((8, half, width), bf16),
            pltpu.VMEM((8, half, width), bf16),
            pltpu.VMEM((8, half, width), bf16),
            pltpu.VMEM((rows, width), bf16),
            pltpu.VMEM((rows, width), f32),
            pltpu.VMEM((2, compact // 2, columns), f32),
            pltpu.VMEM((2, compact // 2, width), f32),
            pltpu.VMEM((8, rows), f32),
            pltpu.VMEM((8, rows), f32),
            pltpu.VMEM((4, 2, share, columns), bf16),
            pltpu.VMEM((4, 2, share, columns), bf16),
            pltpu.VMEM((2, 4, 2, share, columns), bf16),
            pltpu.VMEM((2, compact // 2, width), bf16),
            pltpu.VMEM((2, compact // 2, width), bf16),
            pltpu.VMEM((4, 2, share, columns), bf16),
            pltpu.VMEM((8, 128), f32),
            pltpu.VMEM((7, 8, 128), f32),
            pltpu.VMEM((share, columns), bf16),
            pltpu.VMEM((share, columns), f32),
            *ring_buffers((3 * half // 8, width), (half // 4, width)),
            *ring_buffers((3 * half // 8, width), (half // 4, width)),
            *ring_buffers((share, 3 * columns // 8), (share, columns // 4)),
            *scatter_buffers(share, columns // 2),
            dma((6,)), dma((16,)), dma((2, 8)), dma((2, 8)), dma((9,)), dma((9,)), dma((9,)), dma((9,)),
            dma((9,)), dma((9,)), dma((1,)), dma((1,)), dma((2,)), dma((2,)), dma((7,)), dma((7,)), dma((9,)), dma((9,)), dma((10,)), dma((10,)),
            dma((6,)), dma((1,)),
        ],
        compiler_params=pltpu.CompilerParams(collective_id=0, has_side_effects=True, vmem_limit_bytes=62 << 20),
        cost_estimate=pl.CostEstimate(flops=2 * rows * width * D, bytes_accessed=16 << 20, transcendentals=0),
    )(counts, owners, accept_rows, norm_gain[None, :], low_state, mid_state, residual, attention, o_weight, weights, target)
    steps = 4
    top_state, grad = pl.pallas_call(
        grad_kernel,
        grid=(steps,),
        out_shape=(
            jax.ShapeDtypeStruct((rows, width), bf16),
            jax.ShapeDtypeStruct((3 * width, columns), f32),
        ),
        in_specs=[
            pl.BlockSpec((8, rows), lambda i: (0, 0)),
            pl.BlockSpec((rows, width), lambda i: (0, 0)),
            pl.BlockSpec((3 * width // steps, compact), lambda i: (i, 0)),
            pl.BlockSpec((compact, columns), lambda i: (0, 0)),
        ],
        out_specs=(
            pl.BlockSpec((rows // steps, width), lambda i: (i, 0)),
            pl.BlockSpec((3 * width // steps, columns), lambda i: (i, 0)),
        ),
        compiler_params=pltpu.CompilerParams(vmem_limit_bytes=62 << 20),
        cost_estimate=pl.CostEstimate(flops=6 * width * compact * columns, bytes_accessed=12 << 20, transcendentals=0),
    )(accept_rows, top_perm, turned, back.reshape(compact, columns))
    return (top_state, grad.reshape(fc_weight.shape))


def solution(mesh):
    in_specs = (
        P("group", "tensor"),
        P("group", "tensor"),
        P("group", "tensor"),
        P("group", "tensor"),
        P("tensor", None),
        P(None, "tensor", "group"),
        P("group"),
        P("tensor", "group"),
        P(),
        P(),
        P(),
    )
    out_specs = (P("group", "tensor"), P(None, "tensor", "group"))
    return jax.shard_map(shards, mesh=mesh, in_specs=in_specs, out_specs=out_specs, check_vma=False)
```

```python
import jax
import jax.numpy as jnp
from jax import lax
from jax.experimental import pallas as pl
from jax.experimental.pallas import tpu as pltpu
from jax.sharding import PartitionSpec as P

D = 8192
SLOTS = 32
MESH = pl.DeviceIdType.MESH

epsilon = 1e-05


def place_in_mesh():
    group, tensor = lax.axis_index("group"), lax.axis_index("tensor")
    return group // 2, group % 2, tensor // 4, (tensor // 2) % 2, tensor % 2


def device(z, low, y, high, core):
    return (z * 2 + low, y * 4 + high * 2 + core)


def send(src, dst, send_sem, recv_sem, peer):
    return pltpu.make_async_remote_copy(
        src_ref=src, dst_ref=dst, send_sem=send_sem, recv_sem=recv_sem,
        device_id=peer, device_id_type=MESH,
    )


class RingGather:
    def __init__(self, block, other, up, down, sends, recvs):
        self.block, self.other, self.up, self.down = block, other, up, down
        self.sends, self.recvs = sends, recvs
        self.started = []

    def _go(self, at, k, peer, view):
        copy = send(self.block(*at, (0, 0)), self.block(*at, view), self.sends.at[k], self.recvs.at[k], peer)
        copy.start()
        self.started.append(copy)

    def _arrived(self, at, k, peer):
        ref = self.block(*at, (0, 0))
        send(ref, ref, self.sends.at[k], self.recvs.at[k], peer).wait_recv()
        return ref

    def own(self):
        self._go((0, 0, None), 1, self.up, (1, 0))
        self._go((0, 0, None), 2, self.down, (3, 0))
        self._go((0, 0, None), 0, self.other, (0, 1))

    def relay_pair(self):
        ref = self._arrived((0, 1, None), 0, self.other)
        self._go((0, 1, None), 3, self.up, (1, 0))
        self._go((0, 1, None), 4, self.down, (3, 0))
        return [ref]

    def relay_ring(self, flip):
        k = 2 * flip
        low = self._arrived((3, flip, None), 1 + k, self.down)
        self._go((3, flip, 0), 5 + k, self.up, (1, 0))
        high = self._arrived((1, flip, None), 2 + k, self.up)
        self._go((1, flip, 1), 6 + k, self.down, (3, 0))
        return [low, high]

    def last(self, flip):
        k = 2 * flip
        first = self._arrived((2, flip, 0), 5 + k, self.down)
        second = self._arrived((2, flip, 1), 6 + k, self.up)
        return [first, second]

    def drain(self):
        for copy in self.started:
            copy.wait_send()


class RingFirstGather(RingGather):
    def relay_pair(self):
        return [self._arrived((0, 1, None), 0, self.other)]

    def relay_ring(self, flip):
        if flip:
            return [self._arrived((3, 1, None), 3, self.other), self._arrived((1, 1, None), 4, self.other)]
        low = self._arrived((3, 0, None), 1, self.down)
        self._go((3, 0, 0), 5, self.up, (1, 0))
        self._go((3, 0, None), 3, self.other, (0, 1))
        high = self._arrived((1, 0, None), 2, self.up)
        self._go((1, 0, 1), 6, self.down, (3, 0))
        self._go((1, 0, None), 4, self.other, (0, 1))
        return [low, high]

    def last(self, flip):
        if flip:
            return [self._arrived((2, 1, 0), 7, self.other), self._arrived((2, 1, 1), 8, self.other)]
        first = self._arrived((2, 0, 0), 5, self.down)
        self._go((2, 0, 0), 7, self.other, (0, 1))
        second = self._arrived((2, 0, 1), 6, self.up)
        self._go((2, 0, 1), 8, self.other, (0, 1))
        return [first, second]


class ChipScatter:
    def __init__(self, acc, first, second, y, high, peers, partner, bufs, sends, recvs):
        self.acc, self.first, self.second = acc, first, second
        self.y, self.high, self.peers, self.partner = y, high, peers, partner
        self.ya, self.xb, self.xs, self.xa, self.bs, self.yb, self.own = bufs
        self.sends, self.recvs = sends, recvs
        self.copies = {}

    def _go(self, src, dst, k, peer):
        copy = send(src, dst, self.sends.at[k], self.recvs.at[k], peer)
        copy.start()
        self.copies[k] = copy

    def start(self):
        self.start_first()
        self.start_second()

    def start_first(self):
        for d in (1, 2, 3):
            to = (self.y + d) % 4
            self._go(self.acc.at[(to, slice(None), *self.first)], self.ya.at[d - 1], d - 1, self.peers[d - 1])

    def start_second(self):
        self._go(self.acc.at[(slice(None), 1 - self.high, *self.second)], self.xb, 3, self.partner)

    def middle(self):
        for d in (1, 2, 3):
            self.copies[d - 1].wait_recv()

        def along_y(side):
            total = self.acc[(self.y, side, *self.first)].astype(jnp.float32)
            for d in (0, 1, 2):
                total += self.ya[d, side].astype(jnp.float32)
            return total

        self.xs[...] = along_y(1 - self.high).astype(jnp.bfloat16)
        self._go(self.xs, self.xa, 4, self.partner)
        self.own[0] = along_y(self.high)
        self.copies[3].wait_recv()
        for d in (1, 2, 3):
            to = (self.y + d) % 4
            pair = self.acc[(to, self.high, *self.second)].astype(jnp.float32) + self.xb[to].astype(jnp.float32)
            self.bs[d - 1] = pair.astype(jnp.bfloat16)
            self._go(self.bs.at[d - 1], self.yb.at[d - 1], 4 + d, self.peers[d - 1])
        self.own[1] = self.acc[(self.y, self.high, *self.second)].astype(jnp.float32) + self.xb[self.y].astype(jnp.float32)

    def finish(self):
        self.copies[4].wait_recv()
        first = self.own[0] + self.xa[...].astype(jnp.float32)
        total = self.own[1]
        for d in (1, 2, 3):
            self.copies[4 + d].wait_recv()
            total += self.yb[d - 1].astype(jnp.float32)
        return first, total

    def drain(self):
        for copy in self.copies.values():
            copy.wait_send()


class RingScatter:
    def __init__(self, acc, halves, rest, y, high, peers, partner, bufs, sends, recvs):
        self.acc, self.halves, self.rest = acc, halves, rest
        self.y, self.high, self.peers, self.partner = y, high, peers, partner
        self.far, self.sums, self.below, self.above, self.xs, self.xa, self.own, self.xb, self.bs, self.yb, self.kept = bufs
        self.sends, self.recvs = sends, recvs
        self.copies = {}

    def _go(self, src, dst, k, peer):
        copy = send(src, dst, self.sends.at[k], self.recvs.at[k], peer)
        copy.start()
        self.copies[k] = copy

    def _block(self, step, side, half):
        return ((self.y + step) % 4, side, *self.halves[half])

    def start(self):
        both = slice(None)
        up, down = self.peers[0], self.peers[2]
        self._go(self.acc.at[self._block(2, both, 0)], self.far.at[0], 0, up)
        self._go(self.acc.at[self._block(2, both, 1)], self.far.at[1], 1, down)
        self._go(self.acc.at[(both, 1 - self.high, *self.rest)], self.xb, 4, self.partner)
        self._go(self.acc.at[self._block(1, both, 1)], self.below.at[1], 2, up)
        self._go(self.acc.at[self._block(3, both, 0)], self.above.at[0], 3, down)

    def relay(self):
        for half, step, into, peer in ((0, 1, self.below, self.peers[0]), (1, 3, self.above, self.peers[2])):
            self.copies[half].wait_recv()
            for side in (0, 1):
                total = self.acc[self._block(step, side, half)].astype(jnp.float32) + self.far[half, side].astype(jnp.float32)
                self.sums[half, side] = total.astype(jnp.bfloat16)
            self._go(self.sums.at[half], into.at[half], 5 + half, peer)
        self.copies[4].wait_recv()
        for d in (1, 2, 3):
            to = (self.y + d) % 4
            pair = self.acc[(to, self.high, *self.rest)].astype(jnp.float32) + self.xb[to].astype(jnp.float32)
            self.bs[d - 1] = pair.astype(jnp.bfloat16)
            self._go(self.bs.at[d - 1], self.yb.at[d - 1], 7 + d, self.peers[d - 1])
        self.kept[...] = self.acc[(self.y, self.high, *self.rest)].astype(jnp.float32) + self.xb[self.y].astype(jnp.float32)

    def middle(self):
        for k in (2, 3, 5, 6):
            self.copies[k].wait_recv()

        def along_y(side, half):
            total = self.acc[self._block(0, side, half)].astype(jnp.float32)
            return total + self.below[half, side].astype(jnp.float32) + self.above[half, side].astype(jnp.float32)

        for half in (0, 1):
            self.xs[half] = along_y(1 - self.high, half).astype(jnp.bfloat16)
        self._go(self.xs, self.xa, 7, self.partner)
        for half in (0, 1):
            self.own[half] = along_y(self.high, half)

    def finish(self):
        self.copies[7].wait_recv()
        rest = self.kept[...]
        for d in (1, 2, 3):
            self.copies[7 + d].wait_recv()
            rest += self.yb[d - 1].astype(jnp.float32)
        return self.own[0] + self.xa[0].astype(jnp.float32), self.own[1] + self.xa[1].astype(jnp.float32), rest

    def drain(self):
        for copy in self.copies.values():
            copy.wait_send()


def ring_buffers(half, rest):
    bf16, f32 = jnp.bfloat16, jnp.float32
    return [
        pltpu.VMEM((2, 2, *half), bf16),
        pltpu.VMEM((2, 2, *half), bf16),
        pltpu.VMEM((2, 2, *half), bf16),
        pltpu.VMEM((2, 2, *half), bf16),
        pltpu.VMEM((2, *half), bf16),
        pltpu.VMEM((2, *half), bf16),
        pltpu.VMEM((2, *half), f32),
        pltpu.VMEM((4, *rest), bf16),
        pltpu.VMEM((3, *rest), bf16),
        pltpu.VMEM((3, *rest), bf16),
        pltpu.VMEM(rest, f32),
        pltpu.SemaphoreType.DMA((11,)),
        pltpu.SemaphoreType.DMA((11,)),
    ]


def scatter_buffers(rows, columns):
    return [
        pltpu.VMEM((3, 2, rows, columns), jnp.bfloat16),
        pltpu.VMEM((4, rows, columns), jnp.bfloat16),
        pltpu.VMEM((rows, columns), jnp.bfloat16),
        pltpu.VMEM((rows, columns), jnp.bfloat16),
        pltpu.VMEM((3, rows, columns), jnp.bfloat16),
        pltpu.VMEM((3, rows, columns), jnp.bfloat16),
        pltpu.VMEM((2, rows, columns), jnp.float32),
        pltpu.SemaphoreType.DMA((8,)),
        pltpu.SemaphoreType.DMA((8,)),
    ]


def group_block(ref, rows):
    order = {0: 0, 1: 1, 3: 2, 2: 3}

    def block(r, s, half, view):
        slot = order[(r - view[0]) % 4] * 2 + (s ^ view[1])
        if half is None:
            return ref.at[slot]
        return ref.at[slot, pl.ds(half * (rows // 2), rows // 2)]

    return block


def step_kernel(
    counts_ref, owners_ref, accept_ref, gain_ref, low_hbm, mid_hbm, res_hbm, att_hbm, w_hbm, fc_hbm, target_hbm,
    top_ref, xct_ref, back_ref,
    low, mid, res, att, wbuf, fcw, target,
    psend, prec, acc, gl, gm, gt, attp, resp, ylm, topacc, hits, ranks,
    tsend, trecv, tacc, dsend, drecv, dacc, stat, stats, own_back, own_wanted, kept,
    a0, a1, a2, a3, a4, a5, a6, a7, a8, a9, a10, as_, ar_,
    b0, b1, b2, b3, b4, b5, b6, b7, b8, b9, b10, bs_, br_,
    c0, c1, c2, c3, c4, c5, c6, c7, c8, c9, c10, cs_, cr_,
    d0, d1, d2, d3, d4, d5, d6, ds_, dr_,
    e0, e1, e2, e3, e4, e5, e6, es_, er_,
    lsem, wsem, psem, qsem, gsend, grecv, msend, mrecv, hsend, hrecv, tsem, usem, esem, fsem, ssend, srecv, isend, irecv, nsend, nrecv, jsend, jrecv,
    xsem, ksem,
):
    z, xl, y, xh, c = place_in_mesh()
    g, tensor = lax.axis_index("group"), lax.axis_index("tensor")
    bf16, f32 = jnp.bfloat16, jnp.float32
    n_rows, width = att.shape
    half = n_rows // 2
    columns = fcw.shape[1]
    share = own_back.shape[0]
    compact = 16 * share
    mine_half = compact // 2

    small = [
        pltpu.make_async_copy(src, dst, lsem.at[k])
        for k, (src, dst) in enumerate(
            ((low_hbm, low), (mid_hbm, mid), (att_hbm, att), (res_hbm, res), (target_hbm, target), (fc_hbm, fcw))
        )
    ]
    loads = [
        pltpu.make_async_copy(
            w_hbm.at[:, pl.ds(k * width, width)], wbuf.at[:, pl.ds(k * width, width)], wsem.at[k]
        )
        for k in range(16)
    ]
    for load in small[:2]:
        load.start()
    sib = device(z, xl, y, xh, 1 - c)
    partner = device(z, xl, y, 1 - xh, c)
    peers = [device(z, xl, (y + d) % 4, xh, c) for d in (1, 2, 3)]
    other = device(z, 1 - xl, y, xh, c)
    up, down = device((z + 1) % 4, xl, y, xh, c), device((z + 3) % 4, xl, y, xh, c)
    replicas = [((g + d) % 8, tensor) for d in range(1, 8)]
    barrier = pltpu.get_barrier_semaphore()
    for peer in (sib, partner, *peers, *replicas):
        pl.semaphore_signal(barrier, inc=1, device_id=peer, device_id_type=MESH)
    for load in (small[2], *loads, *small[3:]):
        load.start()

    lane8 = lax.broadcasted_iota(jnp.int32, (n_rows, 8), 1)
    order = accept_ref[...].astype(f32).T
    order = jnp.sum(jnp.where(lane8 == g, order, 0.0), axis=1, keepdims=True).astype(jnp.int32)
    pick = (order == lax.broadcasted_iota(jnp.int32, (n_rows, n_rows), 1)).astype(bf16)

    def picked(ref, rows):
        return jnp.dot(pick[:rows], ref[...], preferred_element_type=f32)

    low_part = RingGather(group_block(gl, half), other, up, down, gsend, grecv)
    mid_part = RingGather(group_block(gm, half), other, up, down, msend, mrecv)
    top = RingGather(group_block(gt, half), other, up, down, hsend, hrecv)
    small[0].wait()
    gl[0] = picked(low, half).astype(bf16)
    pl.semaphore_wait(barrier, 5 + len(replicas))
    low_part.own()
    small[1].wait()
    gm[0] = picked(mid, half).astype(bf16)
    mid_part.own()
    small[2].wait()
    attp[...] = picked(att, n_rows).astype(bf16)
    for load in loads:
        load.wait()

    def to_sibling(r, b):
        rows = pl.ds(r * half, half)
        return send(psend.at[b, rows], prec.at[b, rows], psem.at[r, b], qsem.at[r, b], sib)

    def weight(k):
        return wbuf[:, pl.ds(pl.multiple_of(k * width, width), width)]

    def product(r):
        rows = pl.ds(r * half, half)

        def theirs(b, _):
            part = jnp.dot(attp[rows], weight(2 * b + 1 - c), preferred_element_type=f32)
            psend[b, rows] = part.astype(bf16)
            to_sibling(r, b).start()
            return 0

        lax.fori_loop(0, 8, theirs, 0)

        def ours(b, _):
            part = jnp.dot(attp[rows], weight(2 * b + c), preferred_element_type=f32)
            to_sibling(r, b).wait_recv()
            acc[b // 2, b % 2, rows] = (part + prec[b, rows].astype(f32)).astype(bf16)
            return 0

        lax.fori_loop(0, 8, ours, 0)

    cut = 3 * half // 8

    def scatter(into, halves, rest, bufs, sends, recvs):
        return RingScatter(into, halves, rest, y, xh, peers, partner, bufs, sends, recvs)

    def scatter_rows(r, bufs, sends, recvs):
        at = r * half
        return scatter(
            acc, ((pl.ds(at, cut),), (pl.ds(at + cut, cut),)), (pl.ds(at + 2 * cut, half - 2 * cut),), bufs, sends, recvs
        )

    def keep_top(r, sums):
        at = r * half
        for part in sums:
            rows = pl.ds(at, part.shape[0])
            top_ref[rows] = (resp[rows] + part).astype(bf16)
            at += part.shape[0]

    product(0)
    rs0 = scatter_rows(0, (a0, a1, a2, a3, a4, a5, a6, a7, a8, a9, a10), as_, ar_)
    rs0.start()
    low_part.relay_pair()
    product(1)
    mid_part.relay_pair()
    low_part.relay_ring(0)

    owner = tensor // 2
    position = lax.broadcasted_iota(jnp.int32, (8, n_rows), 1)
    replica = lax.broadcasted_iota(jnp.int32, (8, n_rows), 0)
    limit = jnp.zeros((8, n_rows), jnp.int32)
    for k in range(8):
        limit = jnp.where(replica == k, counts_ref[k], limit)
    hit = jnp.where((owners_ref[...] == owner) & (position < limit), 1.0, 0.0).astype(f32)
    before = lax.broadcasted_iota(jnp.int32, (n_rows, n_rows), 0) < lax.broadcasted_iota(jnp.int32, (n_rows, n_rows), 1)
    hits[...] = hit
    ranks[...] = jnp.dot(hit.astype(bf16), before.astype(bf16), preferred_element_type=f32)

    def offset(which):
        total = jnp.int32(0)
        for k in range(8):
            total += jnp.where(k < which, counts_ref[k], 0)
        return total

    rows_of = []
    for k in range(4):
        which = (tensor % 2) * 4 + k
        member = lax.broadcasted_iota(jnp.int32, (SLOTS, n_rows), 0).astype(f32)
        row = (lax.broadcasted_iota(jnp.int32, (SLOTS, n_rows), 1) + offset(which) + 1).astype(f32)
        here = (ranks[pl.ds(which, 1), :] == member) & (hits[pl.ds(which, 1), :] > 0.5)
        rows_of.append(jnp.sum(jnp.where(here, row, 0.0), axis=1, keepdims=True))
    slot_row = jnp.concatenate(rows_of, axis=0).astype(jnp.int32) - 1
    spread = (slot_row == lax.broadcasted_iota(jnp.int32, (4 * SLOTS, compact), 1)).astype(f32).T.astype(bf16)
    small[4].wait()
    placed = jnp.dot(spread, target[...], preferred_element_type=f32).astype(bf16)
    tacc[...] = placed.reshape(2, 4, 2, share, columns)
    swap_target = send(tacc.at[1 - c], trecv, tsem.at[0], usem.at[0], sib)
    swap_target.start()

    rs0.relay()
    low_part.relay_ring(1)
    mid_part.relay_ring(0)
    small[3].wait()
    resp[...] = picked(res, n_rows)

    def sent(b, _):
        to_sibling(0, b).wait_send()
        to_sibling(1, b).wait_send()
        return 0

    lax.fori_loop(0, 8, sent, 0)

    for slot in range(8):
        step = (0, 1, 3, 2)[slot // 2]
        which = ((z + step) % 4) * 2 + (xl ^ (slot % 2))
        count = counts_ref[which]
        start = offset(which)
        for part in range(2):
            column = lax.broadcasted_iota(jnp.int32, (mine_half, half), 1)
            row = lax.broadcasted_iota(jnp.int32, (mine_half, half), 0)
            hot = (row + (part * mine_half) - start == column) & (column < count)
            wbuf[:, pl.ds(part * 8 * half + slot * half, half)] = hot.astype(bf16)
    hot_width = 8 * half
    held = 2 * hot_width
    near = 6 * half

    def place(part, chunk):
        return pl.ds(held + part * 3 * width + chunk * width, width)

    def compact_rows(ref, chunk):
        for part in range(2):
            hot = wbuf[:, pl.ds(part * hot_width, hot_width)]
            rows = ref[...].reshape(hot_width, width)
            wbuf[:, place(part, chunk)] = jnp.dot(hot, rows, preferred_element_type=f32).astype(bf16)

    def product_rows(chunk):
        for part in range(2):
            for side in range(2):
                cols = pl.ds(side * width, width)
                got = jnp.dot(
                    wbuf[:, place(part, chunk)], fcw[chunk * width:(chunk + 1) * width, cols], preferred_element_type=f32
                )
                ylm[part, :, cols] = got if chunk == 0 else ylm[part, :, cols] + got

    turns = []

    def turn(chunk):
        for part in range(2):
            k = chunk * 2 + part
            psend[k] = wbuf[:, place(part, chunk)].T
            copy = pltpu.make_async_copy(
                psend.at[k],
                xct_ref.at[pl.ds(chunk * width, width), pl.ds(part * mine_half, mine_half)],
                xsem.at[k],
            )
            copy.start()
            turns.append(copy)

    rs0.middle()
    swap_target.wait_recv()
    tsend[...] = (tacc[c].astype(f32) + trecv[...].astype(f32)).astype(bf16)
    side = 3 * columns // 8
    every = pl.ds(0, share)
    rst = scatter(
        tsend, ((every, pl.ds(0, side)), (every, pl.ds(side, side))), (every, pl.ds(2 * side, columns - 2 * side)),
        (c0, c1, c2, c3, c4, c5, c6, c7, c8, c9, c10), cs_, cr_,
    )
    rst.start()
    mid_part.relay_ring(1)
    keep_top(0, rs0.finish())
    gt[0] = top_ref[:half]
    top.own()
    rs1 = scatter_rows(1, (b0, b1, b2, b3, b4, b5, b6, b7, b8, b9, b10), bs_, br_)
    rs1.start()
    low_part.last(0)
    low_part.last(1)
    compact_rows(gl, 0)
    rst.relay()
    small[5].wait()
    product_rows(0)
    top.relay_pair()
    rst.middle()
    rs1.relay()
    turn(0)
    mid_part.last(0)
    mid_part.last(1)
    compact_rows(gm, 1)
    top.relay_ring(0)
    product_rows(1)
    turn(1)
    top.relay_ring(1)
    for part in range(2):
        hot = wbuf[:, pl.ds(part * hot_width, near)]
        topacc[part] = jnp.dot(hot, gt[:6].reshape(near, width), preferred_element_type=f32)
    rs1.middle()
    own_wanted[...] = jnp.concatenate(rst.finish(), axis=1)
    top.last(0)
    top.last(1)

    def swap(side):
        return send(dsend.at[side], drecv.at[side], esem.at[side], fsem.at[side], sib)

    def top_rows(part):
        hot = wbuf[:, pl.ds(pl.multiple_of(part * hot_width + near, half), 2 * half)]
        rows = topacc[part] + jnp.dot(hot, gt[6:].reshape(2 * half, width), preferred_element_type=f32)
        rows = rows.astype(bf16)
        wbuf[:, pl.ds(pl.multiple_of(held + part * 3 * width + 2 * width, width), width)] = rows
        return rows

    def features(part, rows, side):
        cols = pl.ds(side * width, width)
        return ylm[part, :, cols] + jnp.dot(rows, fcw[2 * width:, cols], preferred_element_type=f32)

    rows = top_rows(1 - c)
    for side in range(2):
        dsend[side] = features(1 - c, rows, side).astype(bf16)
        swap(side).start()
    piece = share // 2
    rs2 = [
        ChipScatter(
            dacc, (pl.ds(k * piece, piece), pl.ds(0, width)), (pl.ds(k * piece, piece), pl.ds(width, width)),
            y, xh, peers, partner, bufs, sends, recvs,
        )
        for k, (bufs, sends, recvs) in enumerate(
            (((d0, d1, d2, d3, d4, d5, d6), ds_, dr_), ((e0, e1, e2, e3, e4, e5, e6), es_, er_))
        )
    ]
    rows = top_rows(c)
    for side in range(2):
        mine = features(c, rows, side)
        swap(side).wait_recv()
        both = (mine + drecv[side].astype(f32)).astype(bf16)
        dacc[:, :, :, pl.ds(side * width, width)] = both.reshape(4, 2, share, width)
        for part in rs2:
            if side == 0:
                part.start_first()
            else:
                part.start_second()
    for part in rs2:
        part.middle()
    gain = gain_ref[...]
    weight = 1.0 / offset(8).astype(f32)
    copies = []

    def statistics(k):
        combined = jnp.concatenate(rs2[k].finish(), axis=1)
        wanted = own_wanted[k * piece:(k + 1) * piece]
        gained = combined * gain
        lane = lax.broadcasted_iota(jnp.int32, (piece, 128), 1)
        sums = jnp.where(
            lane == 0, jnp.sum(combined * combined, axis=1, keepdims=True),
            jnp.where(
                lane == 1, jnp.sum(gained * gained, axis=1, keepdims=True),
                jnp.sum(gained * wanted, axis=1, keepdims=True),
            ),
        )
        stat[k] = jnp.concatenate([sums, jnp.zeros((128 - piece, 128), f32)], axis=0).T[:8]
        for d in range(1, 8):
            copy = send(stat.at[k], stats.at[k, d - 1], ssend.at[k, d - 1], srecv.at[k, d - 1], replicas[d - 1])
            copy.start()
            copies.append(copy)
        kept[k] = combined

    def backward(k):
        total = stat[k]
        for d in range(7):
            copies[k * 7 + d].wait_recv()
            total += stats[k, d]
        total = jnp.concatenate([total, jnp.zeros((120, 128), f32)], axis=0).T[:piece]
        combined = kept[k]
        wanted = own_wanted[k * piece:(k + 1) * piece]
        scale = lax.rsqrt(total[:, 0:1] / D + epsilon)
        inner = weight * (scale * total[:, 1:2] - total[:, 2:3])
        slope = weight * (combined * gain * scale - wanted)
        back = scale * gain * slope - combined * (scale * scale * scale * inner / D)
        own_back[k * piece:(k + 1) * piece] = back.astype(bf16)

    def back_at(k, r, s, part, core):
        chip = ((y + r) % 4) * 2 + (xh + s) % 2
        if part is None:
            return back_ref.at[core, chip, pl.ds(k * piece, piece)]
        return back_ref.at[core, chip, pl.ds(k * piece + part * (piece // 2), piece // 2)]

    def own_rows(k):
        return own_back.at[pl.ds(k * piece, piece)]

    def back_gather(kind, k, sends, recvs):
        def block(r, s, part, view):
            if (r, s) == (0, 0) and view == (0, 0):
                return own_rows(k)
            return back_at(k, r, s, part, c)

        return kind(block, partner, peers[0], peers[2], sends, recvs)

    ag = [back_gather(RingGather, 0, isend, irecv), back_gather(RingFirstGather, 1, nsend, nrecv)]
    over = [[], []]

    def across(k, src, ref):
        n = len(over[k])
        copy = send(src, ref, jsend.at[k, n], jrecv.at[k, n], sib)
        copy.start()
        over[k].append(copy)

    keeps = [
        pltpu.make_async_copy(own_rows(k), back_at(k, 0, 0, None, c), ksem.at[k]) for k in range(2)
    ]
    for k in range(2):
        statistics(k)
    for k in range(2):
        backward(k)
        ag[k].own()
        across(k, own_rows(k), back_at(k, 0, 0, None, c))
        keeps[k].start()
    for k in range(2):
        for ref in ag[k].relay_pair():
            across(k, ref, ref)
    for flip in (0, 1):
        for k in range(2):
            for ref in ag[k].relay_ring(flip):
                across(k, ref, ref)
    turn(2)
    keep_top(1, rs1.finish())
    for flip in (0, 1):
        for k in range(2):
            for ref in ag[k].last(flip):
                across(k, ref, ref)
    landed = [
        (0, 0, None), (0, 1, None), (3, 0, None), (1, 0, None), (3, 1, None), (1, 1, None),
        (2, 0, 0), (2, 0, 1), (2, 1, 0), (2, 1, 1),
    ]
    for n, at in enumerate(landed):
        for k in range(2):
            ref = back_at(k, *at, 1 - c)
            send(ref, ref, jsend.at[k, n], jrecv.at[k, n], sib).wait_recv()
    for copy in (*copies, *over[0], *over[1], swap(0), swap(1), swap_target):
        copy.wait_send()
    for part in (low_part, mid_part, top, *ag, rs0, rs1, rst, *rs2):
        part.drain()
    for copy in (*turns, *keeps):
        copy.wait()


def grad_kernel(accept_ref, top_ref, x_ref, back_ref, top_state_ref, grad_ref):
    g = lax.axis_index("group")
    rows = top_state_ref.shape[0]
    first = pl.program_id(0) * rows
    row = lax.broadcasted_iota(jnp.int32, (rows, top_ref.shape[0]), 0) + first
    put = (accept_ref[pl.ds(g, 1), :] == row).astype(jnp.bfloat16)
    top_state_ref[...] = jnp.dot(put, top_ref[...], preferred_element_type=jnp.float32).astype(jnp.bfloat16)
    grad_ref[...] = jnp.dot(x_ref[...], back_ref[...], preferred_element_type=jnp.float32)


def shards(
    low_state, mid_state, residual, attention, o_weight, fc_weight, norm_gain, target, counts, accept_rows, owners,
):
    rows, width = attention.shape
    half = rows // 2
    share, columns = target.shape[0] // 2, target.shape[1]
    compact = 16 * share
    vmem = pl.BlockSpec(memory_space=pltpu.VMEM)
    anywhere = pl.BlockSpec(memory_space=pl.ANY)
    dma = pltpu.SemaphoreType.DMA
    bf16, f32 = jnp.bfloat16, jnp.float32
    weights = fc_weight.reshape(3 * width, columns)
    top_perm, turned, back = pl.pallas_call(
        step_kernel,
        out_shape=(
            jax.ShapeDtypeStruct((rows, width), bf16),
            jax.ShapeDtypeStruct((3 * width, compact), bf16),
            jax.ShapeDtypeStruct((2, 8, share, columns), bf16),
        ),
        in_specs=[pl.BlockSpec(memory_space=pltpu.SMEM), vmem, vmem, vmem, *[anywhere] * 7],
        out_specs=(vmem, anywhere, anywhere),
        scratch_shapes=[
            pltpu.VMEM((rows, width), bf16),
            pltpu.VMEM((rows, width), bf16),
            pltpu.VMEM((rows, width), bf16),
            pltpu.VMEM((rows, width), bf16),
            pltpu.VMEM((width, D), bf16),
            pltpu.VMEM((3 * width, columns), bf16),
            pltpu.VMEM((2 * share, columns), bf16),
            pltpu.VMEM((8, rows, width), bf16),
            pltpu.VMEM((8, rows, width), bf16),
            pltpu.VMEM((4, 2, rows, width), bf16),
            pltpu.VMEM((8, half, width), bf16),
            pltpu.VMEM((8, half, width), bf16),
            pltpu.VMEM((8, half, width), bf16),
            pltpu.VMEM((rows, width), bf16),
            pltpu.VMEM((rows, width), f32),
            pltpu.VMEM((2, compact // 2, columns), f32),
            pltpu.VMEM((2, compact // 2, width), f32),
            pltpu.VMEM((8, rows), f32),
            pltpu.VMEM((8, rows), f32),
            pltpu.VMEM((4, 2, share, columns), bf16),
            pltpu.VMEM((4, 2, share, columns), bf16),
            pltpu.VMEM((2, 4, 2, share, columns), bf16),
            pltpu.VMEM((2, compact // 2, width), bf16),
            pltpu.VMEM((2, compact // 2, width), bf16),
            pltpu.VMEM((4, 2, share, columns), bf16),
            pltpu.VMEM((2, 8, 128), f32),
            pltpu.VMEM((2, 7, 8, 128), f32),
            pltpu.VMEM((share, columns), bf16),
            pltpu.VMEM((share, columns), f32),
            pltpu.VMEM((2, share // 2, columns), f32),
            *ring_buffers((3 * half // 8, width), (half // 4, width)),
            *ring_buffers((3 * half // 8, width), (half // 4, width)),
            *ring_buffers((share, 3 * columns // 8), (share, columns // 4)),
            *scatter_buffers(share // 2, columns // 2),
            *scatter_buffers(share // 2, columns // 2),
            dma((6,)), dma((16,)), dma((2, 8)), dma((2, 8)), dma((9,)), dma((9,)), dma((9,)), dma((9,)),
            dma((9,)), dma((9,)), dma((1,)), dma((1,)), dma((2,)), dma((2,)), dma((2, 7)), dma((2, 7)),
            dma((9,)), dma((9,)), dma((9,)), dma((9,)), dma((2, 10)), dma((2, 10)), dma((6,)), dma((2,)),
        ],
        compiler_params=pltpu.CompilerParams(collective_id=0, has_side_effects=True, vmem_limit_bytes=62 << 20),
        cost_estimate=pl.CostEstimate(flops=2 * rows * width * D, bytes_accessed=16 << 20, transcendentals=0),
    )(counts, owners, accept_rows, norm_gain[None, :], low_state, mid_state, residual, attention, o_weight, weights, target)
    steps = 4
    top_state, grad = pl.pallas_call(
        grad_kernel,
        grid=(steps,),
        out_shape=(
            jax.ShapeDtypeStruct((rows, width), bf16),
            jax.ShapeDtypeStruct((3 * width, columns), f32),
        ),
        in_specs=[
            pl.BlockSpec((8, rows), lambda i: (0, 0)),
            pl.BlockSpec((rows, width), lambda i: (0, 0)),
            pl.BlockSpec((3 * width // steps, compact), lambda i: (i, 0)),
            pl.BlockSpec((compact, columns), lambda i: (0, 0)),
        ],
        out_specs=(
            pl.BlockSpec((rows // steps, width), lambda i: (i, 0)),
            pl.BlockSpec((3 * width // steps, columns), lambda i: (i, 0)),
        ),
        compiler_params=pltpu.CompilerParams(vmem_limit_bytes=62 << 20),
        cost_estimate=pl.CostEstimate(flops=6 * width * compact * columns, bytes_accessed=12 << 20, transcendentals=0),
    )(accept_rows, top_perm, turned, back.reshape(compact, columns))
    return (top_state, grad.reshape(fc_weight.shape))


def solution(mesh):
    in_specs = (
        P("group", "tensor"),
        P("group", "tensor"),
        P("group", "tensor"),
        P("group", "tensor"),
        P("tensor", None),
        P(None, "tensor", "group"),
        P("group"),
        P("tensor", "group"),
        P(),
        P(),
        P(),
    )
    out_specs = (P("group", "tensor"), P(None, "tensor", "group"))
    return jax.shard_map(shards, mesh=mesh, in_specs=in_specs, out_specs=out_specs, check_vma=False)
```

```python
import jax
import jax.numpy as jnp
from jax import lax
from jax.experimental import pallas as pl
from jax.experimental.pallas import tpu as pltpu
from jax.sharding import PartitionSpec as P

D = 8192
SLOTS = 32
MESH = pl.DeviceIdType.MESH

epsilon = 1e-05


def place_in_mesh():
    group, tensor = lax.axis_index("group"), lax.axis_index("tensor")
    return group // 2, group % 2, tensor // 4, (tensor // 2) % 2, tensor % 2


def device(z, low, y, high, core):
    return (z * 2 + low, y * 4 + high * 2 + core)


def send(src, dst, send_sem, recv_sem, peer):
    return pltpu.make_async_remote_copy(
        src_ref=src, dst_ref=dst, send_sem=send_sem, recv_sem=recv_sem,
        device_id=peer, device_id_type=MESH,
    )


class RingGather:
    def __init__(self, block, other, up, down, sends, recvs):
        self.block, self.other, self.up, self.down = block, other, up, down
        self.sends, self.recvs = sends, recvs
        self.started = []

    def _go(self, at, k, peer, view):
        copy = send(self.block(*at, (0, 0)), self.block(*at, view), self.sends.at[k], self.recvs.at[k], peer)
        copy.start()
        self.started.append(copy)

    def _arrived(self, at, k, peer):
        ref = self.block(*at, (0, 0))
        send(ref, ref, self.sends.at[k], self.recvs.at[k], peer).wait_recv()
        return ref

    def own(self):
        self._go((0, 0, None), 1, self.up, (1, 0))
        self._go((0, 0, None), 2, self.down, (3, 0))
        self._go((0, 0, None), 0, self.other, (0, 1))

    def relay_pair(self):
        ref = self._arrived((0, 1, None), 0, self.other)
        self._go((0, 1, None), 3, self.up, (1, 0))
        self._go((0, 1, None), 4, self.down, (3, 0))
        return [ref]

    def relay_ring(self, flip):
        k = 2 * flip
        low = self._arrived((3, flip, None), 1 + k, self.down)
        self._go((3, flip, 0), 5 + k, self.up, (1, 0))
        high = self._arrived((1, flip, None), 2 + k, self.up)
        self._go((1, flip, 1), 6 + k, self.down, (3, 0))
        return [low, high]

    def last(self, flip):
        k = 2 * flip
        first = self._arrived((2, flip, 0), 5 + k, self.down)
        second = self._arrived((2, flip, 1), 6 + k, self.up)
        return [first, second]

    def drain(self):
        for copy in self.started:
            copy.wait_send()


class RingFirstGather(RingGather):
    def relay_pair(self):
        return [self._arrived((0, 1, None), 0, self.other)]

    def relay_ring(self, flip):
        if flip:
            return [self._arrived((3, 1, None), 3, self.other), self._arrived((1, 1, None), 4, self.other)]
        low = self._arrived((3, 0, None), 1, self.down)
        self._go((3, 0, 0), 5, self.up, (1, 0))
        self._go((3, 0, None), 3, self.other, (0, 1))
        high = self._arrived((1, 0, None), 2, self.up)
        self._go((1, 0, 1), 6, self.down, (3, 0))
        self._go((1, 0, None), 4, self.other, (0, 1))
        return [low, high]

    def last(self, flip):
        if flip:
            return [self._arrived((2, 1, 0), 7, self.other), self._arrived((2, 1, 1), 8, self.other)]
        first = self._arrived((2, 0, 0), 5, self.down)
        self._go((2, 0, 0), 7, self.other, (0, 1))
        second = self._arrived((2, 0, 1), 6, self.up)
        self._go((2, 0, 1), 8, self.other, (0, 1))
        return [first, second]


class ChipScatter:
    def __init__(self, acc, first, second, y, high, peers, partner, bufs, sends, recvs):
        self.acc, self.first, self.second = acc, first, second
        self.y, self.high, self.peers, self.partner = y, high, peers, partner
        self.ya, self.xb, self.xs, self.xa, self.bs, self.yb, self.own = bufs
        self.sends, self.recvs = sends, recvs
        self.copies = {}

    def _go(self, src, dst, k, peer):
        copy = send(src, dst, self.sends.at[k], self.recvs.at[k], peer)
        copy.start()
        self.copies[k] = copy

    def start(self):
        self.start_first()
        self.start_second()

    def start_first(self):
        for d in (1, 2, 3):
            to = (self.y + d) % 4
            self._go(self.acc.at[(to, slice(None), *self.first)], self.ya.at[d - 1], d - 1, self.peers[d - 1])

    def start_second(self):
        self._go(self.acc.at[(slice(None), 1 - self.high, *self.second)], self.xb, 3, self.partner)

    def middle(self):
        for d in (1, 2, 3):
            self.copies[d - 1].wait_recv()

        def along_y(side):
            total = self.acc[(self.y, side, *self.first)].astype(jnp.float32)
            for d in (0, 1, 2):
                total += self.ya[d, side].astype(jnp.float32)
            return total

        self.xs[...] = along_y(1 - self.high).astype(jnp.bfloat16)
        self._go(self.xs, self.xa, 4, self.partner)
        self.own[0] = along_y(self.high)
        self.copies[3].wait_recv()
        for d in (1, 2, 3):
            to = (self.y + d) % 4
            pair = self.acc[(to, self.high, *self.second)].astype(jnp.float32) + self.xb[to].astype(jnp.float32)
            self.bs[d - 1] = pair.astype(jnp.bfloat16)
            self._go(self.bs.at[d - 1], self.yb.at[d - 1], 4 + d, self.peers[d - 1])
        self.own[1] = self.acc[(self.y, self.high, *self.second)].astype(jnp.float32) + self.xb[self.y].astype(jnp.float32)

    def finish(self):
        self.copies[4].wait_recv()
        first = self.own[0] + self.xa[...].astype(jnp.float32)
        total = self.own[1]
        for d in (1, 2, 3):
            self.copies[4 + d].wait_recv()
            total += self.yb[d - 1].astype(jnp.float32)
        return first, total

    def drain(self):
        for copy in self.copies.values():
            copy.wait_send()


class RingScatter:
    def __init__(self, acc, halves, rest, y, high, peers, partner, bufs, sends, recvs):
        self.acc, self.halves, self.rest = acc, halves, rest
        self.y, self.high, self.peers, self.partner = y, high, peers, partner
        self.far, self.sums, self.below, self.above, self.xs, self.xa, self.own, self.xb, self.bs, self.yb, self.kept = bufs
        self.sends, self.recvs = sends, recvs
        self.copies = {}

    def _go(self, src, dst, k, peer):
        copy = send(src, dst, self.sends.at[k], self.recvs.at[k], peer)
        copy.start()
        self.copies[k] = copy

    def _block(self, step, side, half):
        return ((self.y + step) % 4, side, *self.halves[half])

    def start(self):
        both = slice(None)
        up, down = self.peers[0], self.peers[2]
        self._go(self.acc.at[self._block(2, both, 0)], self.far.at[0], 0, up)
        self._go(self.acc.at[self._block(2, both, 1)], self.far.at[1], 1, down)
        self._go(self.acc.at[(both, 1 - self.high, *self.rest)], self.xb, 4, self.partner)
        self._go(self.acc.at[self._block(1, both, 1)], self.below.at[1], 2, up)
        self._go(self.acc.at[self._block(3, both, 0)], self.above.at[0], 3, down)

    def relay(self):
        for half, step, into, peer in ((0, 1, self.below, self.peers[0]), (1, 3, self.above, self.peers[2])):
            self.copies[half].wait_recv()
            for side in (0, 1):
                total = self.acc[self._block(step, side, half)].astype(jnp.float32) + self.far[half, side].astype(jnp.float32)
                self.sums[half, side] = total.astype(jnp.bfloat16)
            self._go(self.sums.at[half], into.at[half], 5 + half, peer)
        self.copies[4].wait_recv()
        for d in (1, 2, 3):
            to = (self.y + d) % 4
            pair = self.acc[(to, self.high, *self.rest)].astype(jnp.float32) + self.xb[to].astype(jnp.float32)
            self.bs[d - 1] = pair.astype(jnp.bfloat16)
            self._go(self.bs.at[d - 1], self.yb.at[d - 1], 7 + d, self.peers[d - 1])
        self.kept[...] = self.acc[(self.y, self.high, *self.rest)].astype(jnp.float32) + self.xb[self.y].astype(jnp.float32)

    def middle(self):
        for k in (2, 3, 5, 6):
            self.copies[k].wait_recv()

        def along_y(side, half):
            total = self.acc[self._block(0, side, half)].astype(jnp.float32)
            return total + self.below[half, side].astype(jnp.float32) + self.above[half, side].astype(jnp.float32)

        for half in (0, 1):
            self.xs[half] = along_y(1 - self.high, half).astype(jnp.bfloat16)
        self._go(self.xs, self.xa, 7, self.partner)
        for half in (0, 1):
            self.own[half] = along_y(self.high, half)

    def finish(self):
        self.copies[7].wait_recv()
        rest = self.kept[...]
        for d in (1, 2, 3):
            self.copies[7 + d].wait_recv()
            rest += self.yb[d - 1].astype(jnp.float32)
        return self.own[0] + self.xa[0].astype(jnp.float32), self.own[1] + self.xa[1].astype(jnp.float32), rest

    def drain(self):
        for copy in self.copies.values():
            copy.wait_send()


def ring_buffers(half, rest):
    bf16, f32 = jnp.bfloat16, jnp.float32
    return [
        pltpu.VMEM((2, 2, *half), bf16),
        pltpu.VMEM((2, 2, *half), bf16),
        pltpu.VMEM((2, 2, *half), bf16),
        pltpu.VMEM((2, 2, *half), bf16),
        pltpu.VMEM((2, *half), bf16),
        pltpu.VMEM((2, *half), bf16),
        pltpu.VMEM((2, *half), f32),
        pltpu.VMEM((4, *rest), bf16),
        pltpu.VMEM((3, *rest), bf16),
        pltpu.VMEM((3, *rest), bf16),
        pltpu.VMEM(rest, f32),
        pltpu.SemaphoreType.DMA((11,)),
        pltpu.SemaphoreType.DMA((11,)),
    ]


def scatter_buffers(rows, columns):
    return [
        pltpu.VMEM((3, 2, rows, columns), jnp.bfloat16),
        pltpu.VMEM((4, rows, columns), jnp.bfloat16),
        pltpu.VMEM((rows, columns), jnp.bfloat16),
        pltpu.VMEM((rows, columns), jnp.bfloat16),
        pltpu.VMEM((3, rows, columns), jnp.bfloat16),
        pltpu.VMEM((3, rows, columns), jnp.bfloat16),
        pltpu.VMEM((2, rows, columns), jnp.float32),
        pltpu.SemaphoreType.DMA((8,)),
        pltpu.SemaphoreType.DMA((8,)),
    ]


def group_block(ref, rows):
    order = {0: 0, 1: 1, 3: 2, 2: 3}

    def block(r, s, half, view):
        slot = order[(r - view[0]) % 4] * 2 + (s ^ view[1])
        if half is None:
            return ref.at[slot]
        return ref.at[slot, pl.ds(half * (rows // 2), rows // 2)]

    return block


def step_kernel(
    counts_ref, owners_ref, accept_ref, gain_ref, low_hbm, mid_hbm, res_hbm, att_hbm, w_hbm, fc_hbm, target_hbm,
    top_ref, xct_ref, back_ref,
    low, mid, res, att, wbuf, fcw, target,
    psend, prec, acc, gl, gm, gt, attp, resp, ylm, topacc, hits, ranks,
    tsend, trecv, tacc, dsend, drecv, dacc, stat, stats, own_back, own_wanted, kept,
    a0, a1, a2, a3, a4, a5, a6, a7, a8, a9, a10, as_, ar_,
    b0, b1, b2, b3, b4, b5, b6, b7, b8, b9, b10, bs_, br_,
    c0, c1, c2, c3, c4, c5, c6, c7, c8, c9, c10, cs_, cr_,
    d0, d1, d2, d3, d4, d5, d6, ds_, dr_,
    e0, e1, e2, e3, e4, e5, e6, es_, er_,
    lsem, wsem, psem, qsem, gsend, grecv, msend, mrecv, hsend, hrecv, tsem, usem, esem, fsem, ssend, srecv, isend, irecv, nsend, nrecv, jsend, jrecv,
    xsem, ksem,
):
    z, xl, y, xh, c = place_in_mesh()
    g, tensor = lax.axis_index("group"), lax.axis_index("tensor")
    bf16, f32 = jnp.bfloat16, jnp.float32
    n_rows, width = att.shape
    half = n_rows // 2
    columns = fcw.shape[1]
    share = own_back.shape[0]
    compact = 16 * share
    mine_half = compact // 2

    small = [
        pltpu.make_async_copy(src, dst, lsem.at[k])
        for k, (src, dst) in enumerate(
            ((low_hbm, low), (mid_hbm, mid), (att_hbm, att), (res_hbm, res), (target_hbm, target), (fc_hbm, fcw))
        )
    ]
    loads = [
        pltpu.make_async_copy(
            w_hbm.at[:, pl.ds(k * width, width)], wbuf.at[:, pl.ds(k * width, width)], wsem.at[k]
        )
        for k in range(16)
    ]
    for load in small[:2]:
        load.start()
    sib = device(z, xl, y, xh, 1 - c)
    partner = device(z, xl, y, 1 - xh, c)
    peers = [device(z, xl, (y + d) % 4, xh, c) for d in (1, 2, 3)]
    other = device(z, 1 - xl, y, xh, c)
    up, down = device((z + 1) % 4, xl, y, xh, c), device((z + 3) % 4, xl, y, xh, c)
    replicas = [((g + d) % 8, tensor) for d in range(1, 8)]
    barrier = pltpu.get_barrier_semaphore()
    for peer in (sib, partner, *peers, *replicas):
        pl.semaphore_signal(barrier, inc=1, device_id=peer, device_id_type=MESH)
    for load in (small[2], *loads, *small[3:]):
        load.start()

    lane8 = lax.broadcasted_iota(jnp.int32, (n_rows, 8), 1)
    order = accept_ref[...].astype(f32).T
    order = jnp.sum(jnp.where(lane8 == g, order, 0.0), axis=1, keepdims=True).astype(jnp.int32)
    pick = (order == lax.broadcasted_iota(jnp.int32, (n_rows, n_rows), 1)).astype(bf16)

    def picked(ref, rows):
        return jnp.dot(pick[:rows], ref[...], preferred_element_type=f32)

    low_part = RingGather(group_block(gl, half), other, up, down, gsend, grecv)
    mid_part = RingGather(group_block(gm, half), other, up, down, msend, mrecv)
    top = RingGather(group_block(gt, half), other, up, down, hsend, hrecv)
    small[0].wait()
    gl[0] = picked(low, half).astype(bf16)
    pl.semaphore_wait(barrier, 5 + len(replicas))
    low_part.own()
    small[1].wait()
    gm[0] = picked(mid, half).astype(bf16)
    mid_part.own()
    small[2].wait()
    attp[...] = picked(att, n_rows).astype(bf16)
    for load in loads:
        load.wait()

    def to_sibling(r, b):
        rows = pl.ds(r * half, half)
        return send(psend.at[b, rows], prec.at[b, rows], psem.at[r, b], qsem.at[r, b], sib)

    def weight(k):
        return wbuf[:, pl.ds(pl.multiple_of(k * width, width), width)]

    def product(r):
        rows = pl.ds(r * half, half)

        def theirs(b, _):
            part = jnp.dot(attp[rows], weight(2 * b + 1 - c), preferred_element_type=f32)
            psend[b, rows] = part.astype(bf16)
            to_sibling(r, b).start()
            return 0

        lax.fori_loop(0, 8, theirs, 0)

        def ours(b, _):
            part = jnp.dot(attp[rows], weight(2 * b + c), preferred_element_type=f32)
            to_sibling(r, b).wait_recv()
            acc[b // 2, b % 2, rows] = (part + prec[b, rows].astype(f32)).astype(bf16)
            return 0

        lax.fori_loop(0, 8, ours, 0)

    cut = 3 * half // 8

    def scatter(into, halves, rest, bufs, sends, recvs):
        return RingScatter(into, halves, rest, y, xh, peers, partner, bufs, sends, recvs)

    def scatter_rows(r, bufs, sends, recvs):
        at = r * half
        return scatter(
            acc, ((pl.ds(at, cut),), (pl.ds(at + cut, cut),)), (pl.ds(at + 2 * cut, half - 2 * cut),), bufs, sends, recvs
        )

    def keep_top(r, sums):
        at = r * half
        for part in sums:
            rows = pl.ds(at, part.shape[0])
            top_ref[rows] = (resp[rows] + part).astype(bf16)
            at += part.shape[0]

    product(0)
    rs0 = scatter_rows(0, (a0, a1, a2, a3, a4, a5, a6, a7, a8, a9, a10), as_, ar_)
    rs0.start()
    low_part.relay_pair()
    product(1)
    mid_part.relay_pair()
    low_part.relay_ring(0)

    owner = tensor // 2
    position = lax.broadcasted_iota(jnp.int32, (8, n_rows), 1)
    replica = lax.broadcasted_iota(jnp.int32, (8, n_rows), 0)
    limit = jnp.zeros((8, n_rows), jnp.int32)
    for k in range(8):
        limit = jnp.where(replica == k, counts_ref[k], limit)
    hit = jnp.where((owners_ref[...] == owner) & (position < limit), 1.0, 0.0).astype(f32)
    before = lax.broadcasted_iota(jnp.int32, (n_rows, n_rows), 0) < lax.broadcasted_iota(jnp.int32, (n_rows, n_rows), 1)
    hits[...] = hit
    ranks[...] = jnp.dot(hit.astype(bf16), before.astype(bf16), preferred_element_type=f32)

    def offset(which):
        total = jnp.int32(0)
        for k in range(8):
            total += jnp.where(k < which, counts_ref[k], 0)
        return total

    rows_of = []
    for k in range(4):
        which = (tensor % 2) * 4 + k
        member = lax.broadcasted_iota(jnp.int32, (SLOTS, n_rows), 0).astype(f32)
        row = (lax.broadcasted_iota(jnp.int32, (SLOTS, n_rows), 1) + offset(which) + 1).astype(f32)
        here = (ranks[pl.ds(which, 1), :] == member) & (hits[pl.ds(which, 1), :] > 0.5)
        rows_of.append(jnp.sum(jnp.where(here, row, 0.0), axis=1, keepdims=True))
    slot_row = jnp.concatenate(rows_of, axis=0).astype(jnp.int32) - 1
    spread = (slot_row == lax.broadcasted_iota(jnp.int32, (4 * SLOTS, compact), 1)).astype(f32).T.astype(bf16)
    small[4].wait()
    placed = jnp.dot(spread, target[...], preferred_element_type=f32).astype(bf16)
    tacc[...] = placed.reshape(2, 4, 2, share, columns)
    swap_target = send(tacc.at[1 - c], trecv, tsem.at[0], usem.at[0], sib)
    swap_target.start()

    rs0.relay()
    low_part.relay_ring(1)
    mid_part.relay_ring(0)
    small[3].wait()
    resp[...] = picked(res, n_rows)

    def sent(b, _):
        to_sibling(0, b).wait_send()
        to_sibling(1, b).wait_send()
        return 0

    lax.fori_loop(0, 8, sent, 0)

    for slot in range(8):
        step = (0, 1, 3, 2)[slot // 2]
        which = ((z + step) % 4) * 2 + (xl ^ (slot % 2))
        count = counts_ref[which]
        start = offset(which)
        for part in range(2):
            column = lax.broadcasted_iota(jnp.int32, (mine_half, half), 1)
            row = lax.broadcasted_iota(jnp.int32, (mine_half, half), 0)
            hot = (row + (part * mine_half) - start == column) & (column < count)
            wbuf[:, pl.ds(part * 8 * half + slot * half, half)] = hot.astype(bf16)
    hot_width = 8 * half
    held = 2 * hot_width
    near = 6 * half

    def place(part, chunk):
        return pl.ds(held + part * 3 * width + chunk * width, width)

    def compact_rows(ref, chunk):
        for part in range(2):
            hot = wbuf[:, pl.ds(part * hot_width, hot_width)]
            rows = ref[...].reshape(hot_width, width)
            wbuf[:, place(part, chunk)] = jnp.dot(hot, rows, preferred_element_type=f32).astype(bf16)

    def product_rows(chunk):
        for part in range(2):
            for side in range(2):
                cols = pl.ds(side * width, width)
                got = jnp.dot(
                    wbuf[:, place(part, chunk)], fcw[chunk * width:(chunk + 1) * width, cols], preferred_element_type=f32
                )
                ylm[part, :, cols] = got if chunk == 0 else ylm[part, :, cols] + got

    turns = []

    def turn(chunk):
        for part in range(2):
            k = chunk * 2 + part
            psend[k] = wbuf[:, place(part, chunk)].T
            copy = pltpu.make_async_copy(
                psend.at[k],
                xct_ref.at[pl.ds(chunk * width, width), pl.ds(part * mine_half, mine_half)],
                xsem.at[k],
            )
            copy.start()
            turns.append(copy)

    rs0.middle()
    swap_target.wait_recv()
    tsend[...] = (tacc[c].astype(f32) + trecv[...].astype(f32)).astype(bf16)
    side = 3 * columns // 8
    every = pl.ds(0, share)
    rst = scatter(
        tsend, ((every, pl.ds(0, side)), (every, pl.ds(side, side))), (every, pl.ds(2 * side, columns - 2 * side)),
        (c0, c1, c2, c3, c4, c5, c6, c7, c8, c9, c10), cs_, cr_,
    )
    rst.start()
    mid_part.relay_ring(1)
    keep_top(0, rs0.finish())
    gt[0] = top_ref[:half]
    top.own()
    rs1 = scatter_rows(1, (b0, b1, b2, b3, b4, b5, b6, b7, b8, b9, b10), bs_, br_)
    rs1.start()
    low_part.last(0)
    low_part.last(1)
    compact_rows(gl, 0)
    rst.relay()
    small[5].wait()
    product_rows(0)
    top.relay_pair()
    rst.middle()
    rs1.relay()
    turn(0)
    mid_part.last(0)
    mid_part.last(1)
    compact_rows(gm, 1)
    top.relay_ring(0)
    product_rows(1)
    turn(1)
    top.relay_ring(1)
    for part in range(2):
        hot = wbuf[:, pl.ds(part * hot_width, near)]
        topacc[part] = jnp.dot(hot, gt[:6].reshape(near, width), preferred_element_type=f32)
    own_wanted[...] = jnp.concatenate(rst.finish(), axis=1)
    top.last(0)
    top.last(1)

    def swap(side):
        return send(dsend.at[side], drecv.at[side], esem.at[side], fsem.at[side], sib)

    def top_rows(part):
        hot = wbuf[:, pl.ds(pl.multiple_of(part * hot_width + near, half), 2 * half)]
        rows = topacc[part] + jnp.dot(hot, gt[6:].reshape(2 * half, width), preferred_element_type=f32)
        rows = rows.astype(bf16)
        wbuf[:, pl.ds(pl.multiple_of(held + part * 3 * width + 2 * width, width), width)] = rows
        return rows

    def features(part, rows, side):
        cols = pl.ds(side * width, width)
        return ylm[part, :, cols] + jnp.dot(rows, fcw[2 * width:, cols], preferred_element_type=f32)

    rows = top_rows(1 - c)
    for side in range(2):
        dsend[side] = features(1 - c, rows, side).astype(bf16)
        swap(side).start()
    piece = share // 2
    rs2 = [
        ChipScatter(
            dacc, (pl.ds(k * piece, piece), pl.ds(0, width)), (pl.ds(k * piece, piece), pl.ds(width, width)),
            y, xh, peers, partner, bufs, sends, recvs,
        )
        for k, (bufs, sends, recvs) in enumerate(
            (((d0, d1, d2, d3, d4, d5, d6), ds_, dr_), ((e0, e1, e2, e3, e4, e5, e6), es_, er_))
        )
    ]
    rows = top_rows(c)
    for side in range(2):
        mine = features(c, rows, side)
        swap(side).wait_recv()
        both = (mine + drecv[side].astype(f32)).astype(bf16)
        dacc[:, :, :, pl.ds(side * width, width)] = both.reshape(4, 2, share, width)
        for part in rs2:
            if side == 0:
                part.start_first()
            else:
                part.start_second()
    for part in rs2:
        part.middle()
    gain = gain_ref[...]
    weight = 1.0 / offset(8).astype(f32)
    copies = []

    def statistics(k):
        combined = jnp.concatenate(rs2[k].finish(), axis=1)
        wanted = own_wanted[k * piece:(k + 1) * piece]
        gained = combined * gain
        lane = lax.broadcasted_iota(jnp.int32, (piece, 128), 1)
        sums = jnp.where(
            lane == 0, jnp.sum(combined * combined, axis=1, keepdims=True),
            jnp.where(
                lane == 1, jnp.sum(gained * gained, axis=1, keepdims=True),
                jnp.sum(gained * wanted, axis=1, keepdims=True),
            ),
        )
        stat[k] = jnp.concatenate([sums, jnp.zeros((128 - piece, 128), f32)], axis=0).T[:8]
        for d in range(1, 8):
            copy = send(stat.at[k], stats.at[k, d - 1], ssend.at[k, d - 1], srecv.at[k, d - 1], replicas[d - 1])
            copy.start()
            copies.append(copy)
        kept[k] = combined

    def backward(k):
        total = stat[k]
        for d in range(7):
            copies[k * 7 + d].wait_recv()
            total += stats[k, d]
        total = jnp.concatenate([total, jnp.zeros((120, 128), f32)], axis=0).T[:piece]
        combined = kept[k]
        wanted = own_wanted[k * piece:(k + 1) * piece]
        scale = lax.rsqrt(total[:, 0:1] / D + epsilon)
        inner = weight * (scale * total[:, 1:2] - total[:, 2:3])
        slope = weight * (combined * gain * scale - wanted)
        back = scale * gain * slope - combined * (scale * scale * scale * inner / D)
        own_back[k * piece:(k + 1) * piece] = back.astype(bf16)

    def back_at(k, r, s, part, core):
        chip = ((y + r) % 4) * 2 + (xh + s) % 2
        if part is None:
            return back_ref.at[core, chip, pl.ds(k * piece, piece)]
        return back_ref.at[core, chip, pl.ds(k * piece + part * (piece // 2), piece // 2)]

    def own_rows(k):
        return own_back.at[pl.ds(k * piece, piece)]

    def back_gather(kind, k, sends, recvs):
        def block(r, s, part, view):
            if (r, s) == (0, 0) and view == (0, 0):
                return own_rows(k)
            return back_at(k, r, s, part, c)

        return kind(block, partner, peers[0], peers[2], sends, recvs)

    ag = [back_gather(RingGather, 0, isend, irecv), back_gather(RingFirstGather, 1, nsend, nrecv)]
    over = [[], []]

    def across(k, src, ref):
        n = len(over[k])
        copy = send(src, ref, jsend.at[k, n], jrecv.at[k, n], sib)
        copy.start()
        over[k].append(copy)

    keeps = [
        pltpu.make_async_copy(own_rows(k), back_at(k, 0, 0, None, c), ksem.at[k]) for k in range(2)
    ]
    for k in range(2):
        statistics(k)
    rs1.middle()
    for k in range(2):
        backward(k)
        ag[k].own()
        across(k, own_rows(k), back_at(k, 0, 0, None, c))
        keeps[k].start()
    for k in range(2):
        for ref in ag[k].relay_pair():
            across(k, ref, ref)
    for flip in (0, 1):
        for k in range(2):
            for ref in ag[k].relay_ring(flip):
                across(k, ref, ref)
    turn(2)
    keep_top(1, rs1.finish())
    for flip in (0, 1):
        for k in range(2):
            for ref in ag[k].last(flip):
                across(k, ref, ref)
    landed = [
        (0, 0, None), (0, 1, None), (3, 0, None), (1, 0, None), (3, 1, None), (1, 1, None),
        (2, 0, 0), (2, 0, 1), (2, 1, 0), (2, 1, 1),
    ]
    for n, at in enumerate(landed):
        for k in range(2):
            ref = back_at(k, *at, 1 - c)
            send(ref, ref, jsend.at[k, n], jrecv.at[k, n], sib).wait_recv()
    for copy in (*copies, *over[0], *over[1], swap(0), swap(1), swap_target):
        copy.wait_send()
    for part in (low_part, mid_part, top, *ag, rs0, rs1, rst, *rs2):
        part.drain()
    for copy in (*turns, *keeps):
        copy.wait()


def grad_kernel(accept_ref, top_ref, x_ref, back_ref, top_state_ref, grad_ref):
    g = lax.axis_index("group")
    rows = top_state_ref.shape[0]
    first = pl.program_id(0) * rows
    row = lax.broadcasted_iota(jnp.int32, (rows, top_ref.shape[0]), 0) + first
    put = (accept_ref[pl.ds(g, 1), :] == row).astype(jnp.bfloat16)
    top_state_ref[...] = jnp.dot(put, top_ref[...], preferred_element_type=jnp.float32).astype(jnp.bfloat16)
    grad_ref[...] = jnp.dot(x_ref[...], back_ref[...], preferred_element_type=jnp.float32)


def shards(
    low_state, mid_state, residual, attention, o_weight, fc_weight, norm_gain, target, counts, accept_rows, owners,
):
    rows, width = attention.shape
    half = rows // 2
    share, columns = target.shape[0] // 2, target.shape[1]
    compact = 16 * share
    vmem = pl.BlockSpec(memory_space=pltpu.VMEM)
    anywhere = pl.BlockSpec(memory_space=pl.ANY)
    dma = pltpu.SemaphoreType.DMA
    bf16, f32 = jnp.bfloat16, jnp.float32
    weights = fc_weight.reshape(3 * width, columns)
    top_perm, turned, back = pl.pallas_call(
        step_kernel,
        out_shape=(
            jax.ShapeDtypeStruct((rows, width), bf16),
            jax.ShapeDtypeStruct((3 * width, compact), bf16),
            jax.ShapeDtypeStruct((2, 8, share, columns), bf16),
        ),
        in_specs=[pl.BlockSpec(memory_space=pltpu.SMEM), vmem, vmem, vmem, *[anywhere] * 7],
        out_specs=(vmem, anywhere, anywhere),
        scratch_shapes=[
            pltpu.VMEM((rows, width), bf16),
            pltpu.VMEM((rows, width), bf16),
            pltpu.VMEM((rows, width), bf16),
            pltpu.VMEM((rows, width), bf16),
            pltpu.VMEM((width, D), bf16),
            pltpu.VMEM((3 * width, columns), bf16),
            pltpu.VMEM((2 * share, columns), bf16),
            pltpu.VMEM((8, rows, width), bf16),
            pltpu.VMEM((8, rows, width), bf16),
            pltpu.VMEM((4, 2, rows, width), bf16),
            pltpu.VMEM((8, half, width), bf16),
            pltpu.VMEM((8, half, width), bf16),
            pltpu.VMEM((8, half, width), bf16),
            pltpu.VMEM((rows, width), bf16),
            pltpu.VMEM((rows, width), f32),
            pltpu.VMEM((2, compact // 2, columns), f32),
            pltpu.VMEM((2, compact // 2, width), f32),
            pltpu.VMEM((8, rows), f32),
            pltpu.VMEM((8, rows), f32),
            pltpu.VMEM((4, 2, share, columns), bf16),
            pltpu.VMEM((4, 2, share, columns), bf16),
            pltpu.VMEM((2, 4, 2, share, columns), bf16),
            pltpu.VMEM((2, compact // 2, width), bf16),
            pltpu.VMEM((2, compact // 2, width), bf16),
            pltpu.VMEM((4, 2, share, columns), bf16),
            pltpu.VMEM((2, 8, 128), f32),
            pltpu.VMEM((2, 7, 8, 128), f32),
            pltpu.VMEM((share, columns), bf16),
            pltpu.VMEM((share, columns), f32),
            pltpu.VMEM((2, share // 2, columns), f32),
            *ring_buffers((3 * half // 8, width), (half // 4, width)),
            *ring_buffers((3 * half // 8, width), (half // 4, width)),
            *ring_buffers((share, 3 * columns // 8), (share, columns // 4)),
            *scatter_buffers(share // 2, columns // 2),
            *scatter_buffers(share // 2, columns // 2),
            dma((6,)), dma((16,)), dma((2, 8)), dma((2, 8)), dma((9,)), dma((9,)), dma((9,)), dma((9,)),
            dma((9,)), dma((9,)), dma((1,)), dma((1,)), dma((2,)), dma((2,)), dma((2, 7)), dma((2, 7)),
            dma((9,)), dma((9,)), dma((9,)), dma((9,)), dma((2, 10)), dma((2, 10)), dma((6,)), dma((2,)),
        ],
        compiler_params=pltpu.CompilerParams(collective_id=0, has_side_effects=True, vmem_limit_bytes=62 << 20),
        cost_estimate=pl.CostEstimate(flops=2 * rows * width * D, bytes_accessed=16 << 20, transcendentals=0),
    )(counts, owners, accept_rows, norm_gain[None, :], low_state, mid_state, residual, attention, o_weight, weights, target)
    steps = 4
    top_state, grad = pl.pallas_call(
        grad_kernel,
        grid=(steps,),
        out_shape=(
            jax.ShapeDtypeStruct((rows, width), bf16),
            jax.ShapeDtypeStruct((3 * width, columns), f32),
        ),
        in_specs=[
            pl.BlockSpec((8, rows), lambda i: (0, 0)),
            pl.BlockSpec((rows, width), lambda i: (0, 0)),
            pl.BlockSpec((3 * width // steps, compact), lambda i: (i, 0)),
            pl.BlockSpec((compact, columns), lambda i: (0, 0)),
        ],
        out_specs=(
            pl.BlockSpec((rows // steps, width), lambda i: (i, 0)),
            pl.BlockSpec((3 * width // steps, columns), lambda i: (i, 0)),
        ),
        compiler_params=pltpu.CompilerParams(vmem_limit_bytes=62 << 20),
        cost_estimate=pl.CostEstimate(flops=6 * width * compact * columns, bytes_accessed=12 << 20, transcendentals=0),
    )(accept_rows, top_perm, turned, back.reshape(compact, columns))
    return (top_state, grad.reshape(fc_weight.shape))


def solution(mesh):
    in_specs = (
        P("group", "tensor"),
        P("group", "tensor"),
        P("group", "tensor"),
        P("group", "tensor"),
        P("tensor", None),
        P(None, "tensor", "group"),
        P("group"),
        P("tensor", "group"),
        P(),
        P(),
        P(),
    )
    out_specs = (P("group", "tensor"), P(None, "tensor", "group"))
    return jax.shard_map(shards, mesh=mesh, in_specs=in_specs, out_specs=out_specs, check_vma=False)
```
